32 devices in a mesh: ctx: 8 (over y, x, core), head: 4 (over z).
Axes of the slice: x: 2, y: 2, z: 4, core: 2. Of those that a mesh axis runs over, the one named last changes fastest.
Arguments:
- row_query: bfloat16 [8192, 3072], P('ctx', 'head'), may hold values from -160 to 160
- row_key: bfloat16 [8192, 3072], P('ctx', 'head'), may hold values from -5 to 5
- row_value: bfloat16 [8192, 3072], P('ctx', 'head'), may hold values from -6 to 6
- row_cotangent: bfloat16 [8192, 3072], P('ctx', 'head'), may hold values from -6 to 6
- row_mask: int32 [64, 9], replicated, may hold values from 0 to 1, as said below
- col_query: bfloat16 [8192, 3072], P('ctx', 'head'), may hold values from -160 to 160
- col_key: bfloat16 [8192, 3072], P('ctx', 'head'), may hold values from -5 to 5
- col_value: bfloat16 [8192, 3072], P('ctx', 'head'), may hold values from -6 to 6
- col_cotangent: bfloat16 [8192, 3072], P('ctx', 'head'), may hold values from -6 to 6
- col_mask: int32 [64, 64], replicated, may hold values from 0 to 1, as said below
Outputs:
- row_output: bfloat16 [8192, 3072], P('ctx', 'head')
- row_dquery: bfloat16 [8192, 3072], P('ctx', 'head')
- row_dkeys: bfloat16 [8192, 3072], P('ctx', 'head')
- row_dvalues: bfloat16 [8192, 3072], P('ctx', 'head')
- col_output: bfloat16 [8192, 3072], P('ctx', 'head')
- col_dquery: bfloat16 [8192, 3072], P('ctx', 'head')
- col_dkeys: bfloat16 [8192, 3072], P('ctx', 'head')
- col_dvalues: bfloat16 [8192, 3072], P('ctx', 'head')
The draws below stay inside these ranges and needn't reach their ends.
Inputs may be any that keep to these rules, and one draw needn't show every extreme that they name: row_mask[r, 4] = 1 for every r, row_mask[r, 3] = 1 for even r and row_mask[r, 5] = 1 for odd r; entries that point outside the grid are ignored. col_mask[r, r] = 1 for every r and col_mask[r, r - 1] = 1 for r >= 1.
All inputs are finite; a program needn't handle non-finite values.
Results may differ from the reference program's by a relative error of at most 0.022.
Values may be sent and summed in bfloat16 or wider, within the bound.
No kernel may reach another device: no remote copies, remote signals or barrier semaphores. Data moves between devices by JAX's collectives and lax.ppermute only.
A program may use at most 192 MiB of HBM per device.

```python
import jax
import jax.numpy as jnp
from jax import lax

HEAD_DIM = 128
ROW_HEADS = 24
COL_HEADS = 24
GRIDC = 128
RBAND = 4
WINDOW = 9
GRIDR = 64
SEQ = 8192


def drawn_pair(key, salt, heads):
    width = heads * HEAD_DIM
    keys_out = jnp.clip(jax.random.normal(jax.random.fold_in(key, salt), (SEQ, width), jnp.float32), -5.0, 5.0)
    queries_out = jnp.clip(jax.random.normal(jax.random.fold_in(key, salt + 5), (SEQ, width), jnp.float32), -5.0, 5.0)
    return (keys_out, queries_out)


def draw_row_query(key, part):
    return drawn_pair(key, 100, ROW_HEADS)[1].astype(jnp.bfloat16)


def draw_row_key(key, part):
    return drawn_pair(key, 100, ROW_HEADS)[0].astype(jnp.bfloat16)


def draw_col_query(key, part):
    return drawn_pair(key, 200, COL_HEADS)[1].astype(jnp.bfloat16)


def draw_col_key(key, part):
    return drawn_pair(key, 200, COL_HEADS)[0].astype(jnp.bfloat16)


def draw_row_mask(key, part):
    random_bits = jax.random.randint(jax.random.fold_in(key, 300), (GRIDR, WINDOW), 0, 2)
    offsets = jnp.arange(WINDOW)[None, :]
    parity = (jnp.arange(GRIDR) % 2)[:, None]
    center = offsets == RBAND
    backward = (offsets == RBAND - 1) & (parity == 0)
    forward = (offsets == RBAND + 1) & (parity == 1)
    return jnp.where(center | backward | forward, 1, random_bits).astype(jnp.int32)


def draw_col_mask(key, part):
    random_bits = jax.random.randint(jax.random.fold_in(key, 400), (GRIDR, GRIDR), 0, 2)
    rows_idx = jnp.arange(GRIDR)
    forced = (rows_idx[:, None] == rows_idx[None, :]) | (rows_idx[:, None] == rows_idx[None, :] + 1)
    return jnp.where(forced, 1, random_bits).astype(jnp.int32)


def block_levels(key, shape, pieces, least, high):
    level = 1.0
    for axis_at, shards_of in pieces:
        steps = jax.random.uniform(jax.random.fold_in(jax.random.fold_in(key, 6), axis_at), (shards_of,), jnp.float32, least / len(pieces), high / len(pieces))
        level = level * jnp.repeat(jnp.exp(steps), shape[axis_at] // shards_of).reshape((-1,) + (1,) * (len(shape) - 1 - axis_at))
    return level


def gaussian(key, shape, spread, most, pieces=(), kind=jnp.bfloat16):
    values = spread * jax.random.normal(key, shape, jnp.float32)
    if pieces:
        values = values * block_levels(key, shape, pieces, -0.22, 0.18)
    return jnp.clip(values, -most, most).astype(kind)


def setup_inputs(seed: int = 0) -> dict:
    streams_of = jax.random.split(jax.random.key(seed), 11)
    return {
        "row_query": draw_row_query(jax.random.fold_in(streams_of[10], 71), 0),
        "row_key": draw_row_key(jax.random.fold_in(streams_of[10], 71), 0),
        "row_value": gaussian(streams_of[2], (SEQ, ROW_HEADS * HEAD_DIM), 1.0, 6.0, ((0, 8), (1, 4))),
        "row_cotangent": gaussian(streams_of[3], (SEQ, ROW_HEADS * HEAD_DIM), 1.0, 6.0, ((0, 8), (1, 4))),
        "row_mask": draw_row_mask(jax.random.fold_in(streams_of[10], 71), 0),
        "col_query": draw_col_query(jax.random.fold_in(streams_of[10], 71), 0),
        "col_key": draw_col_key(jax.random.fold_in(streams_of[10], 71), 0),
        "col_value": gaussian(streams_of[7], (SEQ, COL_HEADS * HEAD_DIM), 1.0, 6.0, ((0, 8), (1, 4))),
        "col_cotangent": gaussian(streams_of[8], (SEQ, COL_HEADS * HEAD_DIM), 1.0, 6.0, ((0, 8), (1, 4))),
        "col_mask": draw_col_mask(jax.random.fold_in(streams_of[10], 71), 0),
    }


masked_score = -1.0e30


def attend(queries, key_block, value_block, cotangent, allowed):
    scale = queries.shape[-1] ** -0.5
    scores = jnp.einsum("bnd,bmd->bnm", queries.astype(jnp.float32), key_block.astype(jnp.float32)) * scale
    scores = jnp.where(allowed, scores, masked_score)
    row_max = jnp.max(scores, axis=-1, keepdims=True)
    exp_terms = jnp.where(allowed, jnp.exp(scores - row_max), 0.0)
    attn_prob = exp_terms / jnp.sum(exp_terms, axis=-1, keepdims=True)
    prob_low = attn_prob.astype(jnp.bfloat16)
    output = jnp.einsum("bnm,bmd->bnd", prob_low.astype(jnp.float32), value_block.astype(jnp.float32)).astype(jnp.bfloat16)
    d_prob = jnp.einsum("bnd,bmd->bnm", cotangent.astype(jnp.float32), value_block.astype(jnp.float32))
    delta_sum = jnp.sum(cotangent.astype(jnp.float32) * output.astype(jnp.float32), axis=-1, keepdims=True)
    d_scores = (attn_prob * (d_prob - delta_sum)).astype(jnp.bfloat16)
    grad_query = (jnp.einsum("bnm,bmd->bnd", d_scores.astype(jnp.float32), key_block.astype(jnp.float32)) * scale).astype(jnp.bfloat16)
    grad_keys = jnp.einsum("bnm,bnd->bmd", d_scores.astype(jnp.float32), queries.astype(jnp.float32)) * scale
    grad_values = jnp.einsum("bnm,bnd->bmd", prob_low.astype(jnp.float32), cotangent.astype(jnp.float32))
    return output, grad_query, grad_keys, grad_values


def split_heads(array, heads):
    return array.reshape(GRIDR, GRIDC, heads, HEAD_DIM)


def row_heads(row_query, row_key, row_value, row_cotangent, row_mask):
    stacked = [split_heads(a, ROW_HEADS).transpose(2, 0, 1, 3) for a in (row_query, row_key, row_value, row_cotangent)]
    block_rows = jnp.arange(GRIDR)[:, None] + jnp.arange(WINDOW)[None, :] - RBAND
    valid = (block_rows >= 0) & (block_rows < GRIDR) & (row_mask == 1)
    allowed = jnp.repeat(valid, GRIDC, axis=1)[:, None, :]

    def one_head(operands):
        queries, key_rows, value_rows, cotangent = operands
        pad_keys = jnp.pad(key_rows, ((RBAND, RBAND), (0, 0), (0, 0)))
        pad_values = jnp.pad(value_rows, ((RBAND, RBAND), (0, 0), (0, 0)))
        win_keys = jnp.stack([pad_keys[offset:offset + GRIDR] for offset in range(WINDOW)], 1).reshape(GRIDR, WINDOW * GRIDC, HEAD_DIM)
        win_values = jnp.stack([pad_values[offset:offset + GRIDR] for offset in range(WINDOW)], 1).reshape(GRIDR, WINDOW * GRIDC, HEAD_DIM)
        output, grad_query, grad_keys, grad_values = attend(queries, win_keys, win_values, cotangent, allowed)
        grad_keys = grad_keys.reshape(GRIDR, WINDOW, GRIDC, HEAD_DIM)
        grad_values = grad_values.reshape(GRIDR, WINDOW, GRIDC, HEAD_DIM)
        acc_keys = jnp.zeros((GRIDR + 2 * RBAND, GRIDC, HEAD_DIM), jnp.float32)
        acc_values = jnp.zeros((GRIDR + 2 * RBAND, GRIDC, HEAD_DIM), jnp.float32)
        for offset in range(WINDOW):
            acc_keys = acc_keys.at[offset:offset + GRIDR].add(grad_keys[:, offset])
            acc_values = acc_values.at[offset:offset + GRIDR].add(grad_values[:, offset])
        final_keys = acc_keys[RBAND:RBAND + GRIDR].astype(jnp.bfloat16)
        final_values = acc_values[RBAND:RBAND + GRIDR].astype(jnp.bfloat16)
        return output, grad_query, final_keys, final_values

    results = lax.map(one_head, tuple(stacked))
    return tuple(r.transpose(1, 2, 0, 3).reshape(SEQ, ROW_HEADS * HEAD_DIM) for r in results)


def col_heads(col_query, col_key, col_value, col_cotangent, col_mask):
    stacked = [split_heads(a, COL_HEADS).transpose(2, 1, 0, 3) for a in (col_query, col_key, col_value, col_cotangent)]
    allowed = (col_mask == 1)[None]

    def one_head(operands):
        queries, key_rows, value_rows, cotangent = operands
        output, grad_query, grad_keys, grad_values = attend(queries, key_rows, value_rows, cotangent, allowed)
        return output, grad_query, grad_keys.astype(jnp.bfloat16), grad_values.astype(jnp.bfloat16)

    results = lax.map(one_head, tuple(stacked))
    return tuple(r.transpose(2, 1, 0, 3).reshape(SEQ, COL_HEADS * HEAD_DIM) for r in results)


def reference(row_query, row_key, row_value, row_cotangent, row_mask, col_query, col_key, col_value, col_cotangent, col_mask):
    row_output, row_dquery, row_dkeys, row_dvalues = row_heads(row_query, row_key, row_value, row_cotangent, row_mask)
    col_output, col_dquery, col_dkeys, col_dvalues = col_heads(col_query, col_key, col_value, col_cotangent, col_mask)
    return (row_output, row_dquery, row_dkeys, row_dvalues, col_output, col_dquery, col_dkeys, col_dvalues)
```

```python
import functools

import jax
import jax.numpy as jnp
import numpy as np
from jax import lax
from jax.experimental import pallas as pl
from jax.experimental.pallas import tpu as pltpu
from jax.sharding import PartitionSpec as P

HEAD_DIM = 128
GRIDC = 128
GROUP = 8
MASKED = -1e30
SCALE = HEAD_DIM**-0.5
EXP2_SCALE = SCALE * float(np.log2(np.e))
VMEM = 48 << 20


def contract(a, b, dim_a, dim_b):
    return lax.dot_general(
        a, b, (((dim_a,), (dim_b,)), ((), ())), preferred_element_type=jnp.float32
    )


def attend(queries, cotangent, keys, values, add_bias):
    n_keys, n_queries = keys.shape[0], queries.shape[0]
    scores = add_bias(contract(keys, queries, 1, 1))
    top = jnp.max(scores, axis=0, keepdims=True)
    terms = jnp.exp2((scores - top) * EXP2_SCALE)
    prob = terms * (1.0 / jnp.sum(terms, axis=0, keepdims=True))
    prob_low = prob.astype(jnp.bfloat16)
    output = contract(prob_low, values, 0, 0).astype(jnp.bfloat16)
    product = cotangent.astype(jnp.float32) * output.astype(jnp.float32)
    delta = jnp.sum(product.T, axis=0, keepdims=True)
    d_prob = contract(values, cotangent, 1, 1)
    d_scores = (prob * (d_prob - delta)).astype(jnp.bfloat16)
    grad_query = (contract(d_scores, keys, 0, 0) * SCALE).astype(jnp.bfloat16)
    grad_keys = contract(d_scores, queries, 1, 0)
    grad_values = contract(prob_low, cotangent, 1, 0)
    return output, grad_query, grad_keys, grad_values


def row_kernel(
    band, bias, q, k, v, d, k_lo, v_lo, k_hi, v_hi,
    out, dq, dk, dv, lo, hi, keys, values, acc_k, acc_v,
):
    tokens = q.shape[0]
    rim = k_lo.shape[0]
    for whole, before, own, after in ((keys, k_lo, k, k_hi), (values, v_lo, v, v_hi)):
        whole[:rim] = before[...]
        whole[rim : rim + tokens] = own[...]
        whole[rim + tokens :] = after[...]
    acc_k[...] = jnp.zeros_like(acc_k)
    acc_v[...] = jnp.zeros_like(acc_v)
    blocks = 2 * band + 2
    for pair in range(tokens // (2 * GRIDC)):
        here = pl.ds(pair * 2 * GRIDC, 2 * GRIDC)
        window = pl.ds(pair * 2 * GRIDC, blocks * GRIDC)

        def add_bias(scores):
            shaped = scores.reshape(blocks, GRIDC, 2 * GRIDC)
            return (shaped + bias[pair][:, None, :]).reshape(scores.shape)

        output, grad_query, grad_keys, grad_values = attend(
            q[here], d[here], keys[window], values[window], add_bias
        )
        out[here] = output
        dq[here] = grad_query
        acc_k[window] += grad_keys
        acc_v[window] += grad_values
    for at, (acc, own, factor) in enumerate(((acc_k, dk, SCALE), (acc_v, dv, 1.0))):
        own[...] = acc[rim : rim + tokens] * factor
        lo[at] = (acc[:rim] * factor).astype(lo.dtype)
        hi[at] = (acc[rim + tokens :] * factor).astype(hi.dtype)


def row_attention(bias, q, k, v, d, before, after, band):
    tokens, feat = q.shape
    heads = feat // HEAD_DIM
    rim = band * GRIDC
    tall = pl.BlockSpec((tokens, HEAD_DIM), lambda h: (0, h))
    rims = [pl.BlockSpec((None, rim, HEAD_DIM), lambda h, a=a: (a, 0, h)) for a in range(2)]
    both = pl.BlockSpec((2, rim, HEAD_DIM), lambda h: (0, 0, h))
    padded = tokens + 2 * rim
    pairs = tokens * (2 * band + 2) * GRIDC * heads
    return pl.pallas_call(
        functools.partial(row_kernel, band),
        grid=(heads,),
        in_specs=[pl.BlockSpec(bias.shape, lambda h: (0, 0, 0)), tall, tall, tall, tall, *rims, *rims],
        out_specs=[tall, tall, tall, tall, both, both],
        out_shape=[
            jax.ShapeDtypeStruct(q.shape, jnp.bfloat16),
            jax.ShapeDtypeStruct(q.shape, jnp.bfloat16),
            jax.ShapeDtypeStruct(q.shape, jnp.float32),
            jax.ShapeDtypeStruct(q.shape, jnp.float32),
            jax.ShapeDtypeStruct((2, rim, feat), jnp.bfloat16),
            jax.ShapeDtypeStruct((2, rim, feat), jnp.bfloat16),
        ],
        scratch_shapes=[
            pltpu.VMEM((padded, HEAD_DIM), jnp.bfloat16),
            pltpu.VMEM((padded, HEAD_DIM), jnp.bfloat16),
            pltpu.VMEM((padded, HEAD_DIM), jnp.float32),
            pltpu.VMEM((padded, HEAD_DIM), jnp.float32),
        ],
        compiler_params=pltpu.CompilerParams(vmem_limit_bytes=VMEM),
        cost_estimate=pl.CostEstimate(
            flops=24 * pairs * HEAD_DIM, bytes_accessed=30 * tokens * feat, transcendentals=pairs
        ),
        name="row_heads",
    )(bias, q, k, v, d, before, before, after, after)


def col_kernel(bias, x, first, second):
    shape = (x.shape[0], *x.shape[2:])
    tokens = shape[0] * shape[1] * shape[2]
    q, k, v, d = (x[:, a].reshape(tokens, HEAD_DIM) for a in range(4))
    chunk = min(tokens, 256)
    grad_keys, grad_values = 0.0, 0.0
    outputs, grads = [], []
    for start in range(0, tokens, chunk):
        here = slice(start, start + chunk)
        output, grad_query, more_keys, more_values = attend(
            q[here], d[here], k, v, lambda s: s + bias[:, here]
        )
        grad_keys += more_keys
        grad_values += more_values
        outputs.append(output)
        grads.append(grad_query)
    first[:, 0] = jnp.concatenate(outputs, 0).reshape(shape)
    first[:, 1] = jnp.concatenate(grads, 0).reshape(shape)
    second[:, 0] = (grad_keys * SCALE).astype(jnp.bfloat16).reshape(shape)
    second[:, 1] = grad_values.astype(jnp.bfloat16).reshape(shape)


def col_attention(bias, x):
    n, _, rows, cols, feat = x.shape
    heads = feat // HEAD_DIM
    tokens = n * rows * GROUP
    spec = lambda k: pl.BlockSpec((n, k, rows, GROUP, HEAD_DIM), lambda h, g: (0, 0, 0, g, h))
    half = jax.ShapeDtypeStruct((n, 2, rows, cols, feat), jnp.bfloat16)
    pairs = tokens * tokens * heads * (cols // GROUP)
    return pl.pallas_call(
        col_kernel,
        grid=(heads, cols // GROUP),
        in_specs=[pl.BlockSpec(bias.shape, lambda h, g: (0, 0)), spec(4)],
        out_specs=[spec(2), spec(2)],
        out_shape=[half, half],
        compiler_params=pltpu.CompilerParams(vmem_limit_bytes=VMEM),
        cost_estimate=pl.CostEstimate(
            flops=12 * pairs * HEAD_DIM, bytes_accessed=4 * x.size, transcendentals=pairs
        ),
        name="col_heads",
    )(bias, x)


def pack_kernel(*refs):
    *parts, out = refs
    for a, part in enumerate(parts):
        out[a] = part[...]


def packed(arrays, n):
    tokens, feat = arrays[0].shape
    rows, cols, k = tokens // GRIDC, GRIDC // n, len(arrays)
    return pl.pallas_call(
        pack_kernel,
        grid=(n,),
        in_specs=[pl.BlockSpec((rows, cols, feat), lambda j: (0, j, 0))] * k,
        out_specs=pl.BlockSpec((None, k, rows, cols, feat), lambda j: (j, 0, 0, 0, 0)),
        out_shape=jax.ShapeDtypeStruct((n, k, rows, cols, feat), jnp.bfloat16),
        compiler_params=pltpu.CompilerParams(vmem_limit_bytes=VMEM),
        cost_estimate=pl.CostEstimate(
            flops=0, bytes_accessed=4 * k * tokens * feat, transcendentals=0
        ),
        name="pack",
    )(*(a.reshape(rows, GRIDC, feat) for a in arrays))


def unpack_kernel(x, *parts):
    for a, part in enumerate(parts):
        part[...] = x[a]


def unpacked(x):
    n, k, rows, cols, feat = x.shape
    outs = pl.pallas_call(
        unpack_kernel,
        grid=(n,),
        in_specs=[pl.BlockSpec((None, k, rows, cols, feat), lambda j: (j, 0, 0, 0, 0))],
        out_specs=[pl.BlockSpec((rows, cols, feat), lambda j: (0, j, 0))] * k,
        out_shape=[jax.ShapeDtypeStruct((rows, n * cols, feat), jnp.bfloat16)] * k,
        compiler_params=pltpu.CompilerParams(vmem_limit_bytes=VMEM),
        cost_estimate=pl.CostEstimate(flops=0, bytes_accessed=4 * x.size, transcendentals=0),
        name="unpack",
    )(x)
    return [o.reshape(rows * n * cols, feat) for o in outs]


def passed_along(block, distance):
    devices = range(lax.axis_size("ctx"))
    route = [(i - distance, i) for i in devices if i - distance in devices]
    return lax.ppermute(block, "ctx", route)


def exchanged(x):
    return lax.all_to_all(x, "ctx", 0, 0, tiled=True)


def row_bias(mask, first, rows, band, total):
    mask_rows = lax.dynamic_slice_in_dim(mask, first, rows, 0)
    key_rows = (first + jnp.arange(rows))[:, None] + jnp.arange(2 * band + 1)[None, :] - band
    seen = (key_rows >= 0) & (key_rows < total) & (mask_rows == 1)
    seen = seen.reshape(rows // 2, 2, 2 * band + 1)
    even = jnp.pad(seen[:, 0], ((0, 0), (0, 1)))
    odd = jnp.pad(seen[:, 1], ((0, 0), (1, 0)))
    both = jnp.stack([even, odd], axis=-1)
    return jnp.repeat(jnp.where(both, 0.0, MASKED).astype(jnp.float32), GRIDC, axis=2)


def col_bias(mask):
    seen = (mask.T == 1)[:, None, :, None] & jnp.eye(GROUP, dtype=bool)[None, :, None, :]
    size = mask.shape[0] * GROUP
    return jnp.where(seen, 0.0, MASKED).astype(jnp.float32).reshape(size, size)


def body(
    row_query, row_key, row_value, row_cotangent, row_mask,
    col_query, col_key, col_value, col_cotangent, col_mask,
):
    n = lax.axis_size("ctx")
    tokens = row_query.shape[0]
    rows = tokens // GRIDC
    band = (row_mask.shape[1] - 1) // 2
    rim = band * GRIDC
    first_row = lax.axis_index("ctx") * rows

    after = passed_along(jnp.stack([row_key[:rim], row_value[:rim]]), -1)
    before = passed_along(jnp.stack([row_key[tokens - rim :], row_value[tokens - rim :]]), 1)
    moved = exchanged(packed([col_query, col_key, col_value, col_cotangent], n))

    bias = row_bias(row_mask, first_row, rows, band, rows * n)
    row_output, row_dquery, own_k, own_v, lo, hi = row_attention(
        bias, row_query, row_key, row_value, row_cotangent, before, after, band
    )
    from_next = passed_along(lo, -1).astype(jnp.float32)
    from_prev = passed_along(hi, 1).astype(jnp.float32)

    first, second = col_attention(col_bias(col_mask), moved)
    col_output, col_dquery = unpacked(exchanged(first))
    col_dkeys, col_dvalues = unpacked(exchanged(second))

    row_grads = []
    for at, own in enumerate((own_k, own_v)):
        own = own.at[tokens - rim :].add(from_next[at])
        own = own.at[:rim].add(from_prev[at])
        row_grads.append(own.astype(jnp.bfloat16))
    return (
        row_output, row_dquery, *row_grads,
        col_output, col_dquery, col_dkeys, col_dvalues,
    )


def solution(mesh):
    tokens, whole = P("ctx", "head"), P()
    return jax.shard_map(
        body,
        mesh=mesh,
        in_specs=(tokens,) * 4 + (whole,) + (tokens,) * 4 + (whole,),
        out_specs=(tokens,) * 8,
        check_vma=False,
    )
```

```python
import functools

import jax
import jax.numpy as jnp
import numpy as np
from jax import lax
from jax.experimental import pallas as pl
from jax.experimental.pallas import tpu as pltpu
from jax.sharding import PartitionSpec as P

HEAD_DIM = 128
GRIDC = 128
GROUP = 8
MASKED = -1e30
SCALE = HEAD_DIM**-0.5
EXP2_SCALE = SCALE * float(np.log2(np.e))
VMEM = 60 << 20


def contract(a, b, dim_a, dim_b):
    return lax.dot_general(
        a, b, (((dim_a,), (dim_b,)), ((), ())), preferred_element_type=jnp.float32
    )


def attend(queries, cotangent, keys, values, add_bias):
    n_keys, n_queries = keys.shape[0], queries.shape[0]
    scores = add_bias(contract(keys, queries, 1, 1))
    top = jnp.max(scores, axis=0, keepdims=True)
    terms = jnp.exp2((scores - top) * EXP2_SCALE)
    prob = terms * (1.0 / jnp.sum(terms, axis=0, keepdims=True))
    prob_low = prob.astype(jnp.bfloat16)
    output = contract(prob_low, values, 0, 0).astype(jnp.bfloat16)
    product = cotangent.astype(jnp.float32) * output.astype(jnp.float32)
    delta = jnp.sum(product.T, axis=0, keepdims=True)
    d_prob = contract(values, cotangent, 1, 1)
    d_scores = (prob * (d_prob - delta)).astype(jnp.bfloat16)
    grad_query = (contract(d_scores, keys, 0, 0) * SCALE).astype(jnp.bfloat16)
    grad_keys = contract(d_scores, queries, 1, 0)
    grad_values = contract(prob_low, cotangent, 1, 0)
    return output, grad_query, grad_keys, grad_values


def row_kernel(
    band, first, mask, q, k, v, d, k_lo, v_lo, k_hi, v_hi,
    out, dq, dk, dv, lo, hi, keys, values, acc_k, acc_v,
):
    tokens = q.shape[0]
    rim = k_lo.shape[0]
    for whole, before, own, after in ((keys, k_lo, k, k_hi), (values, v_lo, v, v_hi)):
        whole[:rim] = before[...]
        whole[rim : rim + tokens] = own[...]
        whole[rim + tokens :] = after[...]
    acc_k[...] = jnp.zeros_like(acc_k)
    acc_v[...] = jnp.zeros_like(acc_v)
    blocks = 2 * band + 2
    odd = lax.broadcasted_iota(jnp.int32, (1, 2 * GRIDC), 1) >= GRIDC
    total = mask.shape[0]

    def block_bias(row, block):
        key_row = row - band + block
        inside = (key_row >= 0) & (key_row < total)
        sides = []
        for side in range(2):
            offset = block - side
            seen = inside & (mask[row + side, offset] == 1) if 0 <= offset <= 2 * band else False
            sides.append(jnp.where(seen, 0.0, MASKED).astype(jnp.float32))
        return jnp.where(odd, sides[1], sides[0])

    for pair in range(tokens // (2 * GRIDC)):
        here = pl.ds(pair * 2 * GRIDC, 2 * GRIDC)
        window = pl.ds(pair * 2 * GRIDC, blocks * GRIDC)

        def add_bias(scores):
            return jnp.concatenate(
                [
                    scores[b * GRIDC : (b + 1) * GRIDC] + block_bias(first[0] + 2 * pair, b)
                    for b in range(blocks)
                ],
                axis=0,
            )

        output, grad_query, grad_keys, grad_values = attend(
            q[here], d[here], keys[window], values[window], add_bias
        )
        out[here] = output
        dq[here] = grad_query
        acc_k[window] += grad_keys
        acc_v[window] += grad_values
    for at, (acc, own, factor) in enumerate(((acc_k, dk, SCALE), (acc_v, dv, 1.0))):
        own[...] = acc[rim : rim + tokens] * factor
        lo[at] = (acc[:rim] * factor).astype(lo.dtype)
        hi[at] = (acc[rim + tokens :] * factor).astype(hi.dtype)


def row_attention(first, mask, q, k, v, d, before, after, band):
    tokens, feat = q.shape
    heads = feat // HEAD_DIM
    rim = band * GRIDC
    tall = pl.BlockSpec((tokens, HEAD_DIM), lambda h: (0, h))
    rims = [pl.BlockSpec((None, rim, HEAD_DIM), lambda h, a=a: (a, 0, h)) for a in range(2)]
    both = pl.BlockSpec((2, rim, HEAD_DIM), lambda h: (0, 0, h))
    scalars = pl.BlockSpec(memory_space=pltpu.SMEM)
    padded = tokens + 2 * rim
    pairs = tokens * (2 * band + 2) * GRIDC * heads
    return pl.pallas_call(
        functools.partial(row_kernel, band),
        grid=(heads,),
        in_specs=[scalars, scalars, tall, tall, tall, tall, *rims, *rims],
        out_specs=[tall, tall, tall, tall, both, both],
        out_shape=[
            jax.ShapeDtypeStruct(q.shape, jnp.bfloat16),
            jax.ShapeDtypeStruct(q.shape, jnp.bfloat16),
            jax.ShapeDtypeStruct(q.shape, jnp.float32),
            jax.ShapeDtypeStruct(q.shape, jnp.float32),
            jax.ShapeDtypeStruct((2, rim, feat), jnp.bfloat16),
            jax.ShapeDtypeStruct((2, rim, feat), jnp.bfloat16),
        ],
        scratch_shapes=[
            pltpu.VMEM((padded, HEAD_DIM), jnp.bfloat16),
            pltpu.VMEM((padded, HEAD_DIM), jnp.bfloat16),
            pltpu.VMEM((padded, HEAD_DIM), jnp.float32),
            pltpu.VMEM((padded, HEAD_DIM), jnp.float32),
        ],
        compiler_params=pltpu.CompilerParams(vmem_limit_bytes=VMEM),
        cost_estimate=pl.CostEstimate(
            flops=240 * pairs * HEAD_DIM, bytes_accessed=30 * tokens * feat, transcendentals=pairs
        ),
        name="row_heads",
    )(first, mask, q, k, v, d, before, before, after, after)


def col_kernel(mask, x, earlier, first, second, bias):
    del earlier
    @pl.when((pl.program_id(0) == 0) & (pl.program_id(1) == 0))
    def _():
        size, total = bias.shape[0], mask.shape[0]
        row_of = lax.broadcasted_iota(jnp.int32, (size, total), 0) // GROUP
        spread = (row_of == lax.broadcasted_iota(jnp.int32, (size, total), 1)).astype(jnp.bfloat16)
        seen = (mask[...] == 1).astype(jnp.bfloat16)
        by_key = contract(spread, seen, 1, 1).astype(jnp.bfloat16)
        allowed = contract(by_key, spread, 1, 1)
        key_col = lax.broadcasted_iota(jnp.int32, (size, size), 0) % GROUP
        query_col = lax.broadcasted_iota(jnp.int32, (size, size), 1) % GROUP
        bias[...] = jnp.where((key_col == query_col) & (allowed > 0.5), 0.0, MASKED)

    shape = (x.shape[0], *x.shape[2:])
    tokens = shape[0] * shape[1] * shape[2]
    q, k, v, d = (x[:, a].reshape(tokens, HEAD_DIM) for a in range(4))
    chunk = min(tokens, 256)
    grad_keys, grad_values = 0.0, 0.0
    outputs, grads = [], []
    for start in range(0, tokens, chunk):
        here = slice(start, start + chunk)
        output, grad_query, more_keys, more_values = attend(
            q[here], d[here], k, v, lambda s: s + bias[:, here]
        )
        grad_keys += more_keys
        grad_values += more_values
        outputs.append(output)
        grads.append(grad_query)
    first[:, 0] = jnp.concatenate(outputs, 0).reshape(shape)
    first[:, 1] = jnp.concatenate(grads, 0).reshape(shape)
    second[:, 0] = (grad_keys * SCALE).astype(jnp.bfloat16).reshape(shape)
    second[:, 1] = grad_values.astype(jnp.bfloat16).reshape(shape)


def col_attention(mask, x, earlier):
    n, _, rows, cols, feat = x.shape
    heads = feat // HEAD_DIM
    tokens = n * rows * GROUP
    spec = lambda k: pl.BlockSpec((n, k, rows, GROUP, HEAD_DIM), lambda h, g: (0, 0, 0, g, h))
    half = jax.ShapeDtypeStruct((n, 2, rows, cols, feat), jnp.bfloat16)
    pairs = tokens * tokens * heads * (cols // GROUP)
    return pl.pallas_call(
        col_kernel,
        grid=(heads, cols // GROUP),
        in_specs=[
            pl.BlockSpec(mask.shape, lambda h, g: (0, 0)), spec(4), pl.BlockSpec(memory_space=pl.ANY)
        ],
        out_specs=[spec(2), spec(2)],
        out_shape=[half, half],
        scratch_shapes=[pltpu.VMEM((tokens, tokens), jnp.float32)],
        compiler_params=pltpu.CompilerParams(vmem_limit_bytes=VMEM),
        cost_estimate=pl.CostEstimate(
            flops=240 * pairs * HEAD_DIM, bytes_accessed=4 * x.size, transcendentals=pairs
        ),
        name="col_heads",
    )(mask, x, earlier)


def pack_kernel(*refs):
    *parts, out = refs
    for a, part in enumerate(parts):
        out[a] = part[...]


def packed(arrays, n):
    tokens, feat = arrays[0].shape
    rows, cols, k = tokens // GRIDC, GRIDC // n, len(arrays)
    return pl.pallas_call(
        pack_kernel,
        grid=(n,),
        in_specs=[pl.BlockSpec((rows, cols, feat), lambda j: (0, j, 0))] * k,
        out_specs=pl.BlockSpec((None, k, rows, cols, feat), lambda j: (j, 0, 0, 0, 0)),
        out_shape=jax.ShapeDtypeStruct((n, k, rows, cols, feat), jnp.bfloat16),
        compiler_params=pltpu.CompilerParams(vmem_limit_bytes=VMEM),
        cost_estimate=pl.CostEstimate(
            flops=0, bytes_accessed=4 * k * tokens * feat, transcendentals=0
        ),
        name="pack",
    )(*(a.reshape(rows, GRIDC, feat) for a in arrays))


def unpack_kernel(x, *parts):
    for a, part in enumerate(parts):
        part[...] = x[a]


def unpacked(x):
    n, k, rows, cols, feat = x.shape
    outs = pl.pallas_call(
        unpack_kernel,
        grid=(n,),
        in_specs=[pl.BlockSpec((None, k, rows, cols, feat), lambda j: (j, 0, 0, 0, 0))],
        out_specs=[pl.BlockSpec((rows, cols, feat), lambda j: (0, j, 0))] * k,
        out_shape=[jax.ShapeDtypeStruct((rows, n * cols, feat), jnp.bfloat16)] * k,
        compiler_params=pltpu.CompilerParams(vmem_limit_bytes=VMEM),
        cost_estimate=pl.CostEstimate(flops=0, bytes_accessed=4 * x.size, transcendentals=0),
        name="unpack",
    )(x)
    return [o.reshape(rows * n * cols, feat) for o in outs]


def passed_along(block, distance):
    devices = range(lax.axis_size("ctx"))
    route = [(i - distance, i) for i in devices if i - distance in devices]
    return lax.ppermute(block, "ctx", route)


def exchanged(x):
    return lax.all_to_all(x, "ctx", 0, 0, tiled=True)


def body(
    row_query, row_key, row_value, row_cotangent, row_mask,
    col_query, col_key, col_value, col_cotangent, col_mask,
):
    n = lax.axis_size("ctx")
    tokens = row_query.shape[0]
    rows = tokens // GRIDC
    band = (row_mask.shape[1] - 1) // 2
    rim = band * GRIDC
    first_row = lax.axis_index("ctx") * rows

    tops = jnp.stack([row_key[:rim], row_value[:rim]])
    ends = jnp.stack([row_key[tokens - rim :], row_value[tokens - rim :]])
    cols = [col_query, col_key, col_value, col_cotangent]
    tops, ends, *cols = lax.optimization_barrier((tops, ends, *cols))
    after, before = passed_along(tops, -1), passed_along(ends, 1)
    moved = exchanged(packed(cols, n))

    row_output, row_dquery, own_k, own_v, lo, hi = row_attention(
        first_row.reshape(1), row_mask, row_query, row_key, row_value, row_cotangent, before, after, band
    )
    from_next, from_prev = passed_along(lo, -1), passed_along(hi, 1)

    first, second = col_attention(col_mask, moved, row_output)
    first, second, from_next, from_prev = lax.optimization_barrier(
        (first, second, from_next, from_prev)
    )
    col_output, col_dquery = unpacked(exchanged(first))
    col_dkeys, col_dvalues = unpacked(exchanged(second))

    row_grads = []
    for at, own in enumerate((own_k, own_v)):
        own = own.at[tokens - rim :].add(from_next[at].astype(jnp.float32))
        own = own.at[:rim].add(from_prev[at].astype(jnp.float32))
        row_grads.append(own.astype(jnp.bfloat16))
    return (
        row_output, row_dquery, *row_grads,
        col_output, col_dquery, col_dkeys, col_dvalues,
    )


def solution(mesh):
    tokens, whole = P("ctx", "head"), P()
    return jax.shard_map(
        body,
        mesh=mesh,
        in_specs=(tokens,) * 4 + (whole,) + (tokens,) * 4 + (whole,),
        out_specs=(tokens,) * 8,
        check_vma=False,
    )
```

```python
import functools
import math

import jax
import jax.numpy as jnp
import numpy as np
from jax import lax
from jax.experimental import pallas as pl
from jax.experimental.pallas import tpu as pltpu
from jax.sharding import PartitionSpec as P

HEAD_DIM = 128
GRIDC = 128
GROUP = 8
MASKED = -1e30
SCALE = HEAD_DIM**-0.5
EXP2_SCALE = SCALE * float(np.log2(np.e))
VMEM = 60 << 20
CHIPS_APART = 4


def contract(a, b, dim_a, dim_b):
    return lax.dot_general(
        a, b, (((dim_a,), (dim_b,)), ((), ())), preferred_element_type=jnp.float32
    )


def attend(queries, cotangent, keys, values, add_bias):
    n_keys, n_queries = keys.shape[0], queries.shape[0]
    scores = add_bias(contract(keys, queries, 1, 1))
    top = jnp.max(scores, axis=0, keepdims=True)
    terms = jnp.exp2((scores - top) * EXP2_SCALE)
    prob = terms * (1.0 / jnp.sum(terms, axis=0, keepdims=True))
    prob_low = prob.astype(jnp.bfloat16)
    output = contract(prob_low, values, 0, 0).astype(jnp.bfloat16)
    product = cotangent.astype(jnp.float32) * output.astype(jnp.float32)
    delta = jnp.sum(product.T, axis=0, keepdims=True)
    d_prob = contract(values, cotangent, 1, 1)
    d_scores = (prob * (d_prob - delta)).astype(jnp.bfloat16)
    grad_query = (contract(d_scores, keys, 0, 0) * SCALE).astype(jnp.bfloat16)
    grad_keys = contract(d_scores, queries, 1, 0)
    grad_values = contract(prob_low, cotangent, 1, 0)
    return output, grad_query, grad_keys, grad_values


def row_kernel(
    band, place, mask, q, k, v, d, k_lo, v_lo, k_hi, v_hi, v_far,
    out, dq, dk, dv, lo_k, lo_v, hi_k, hi_v, keys, values, acc_k, acc_v,
):
    tokens = q.shape[0]
    rim = k_lo.shape[0]
    for whole, before, own, after in ((keys, k_lo, k, k_hi), (values, v_lo, v, v_hi)):
        whole[:rim] = before[...]
        whole[rim : rim + tokens] = own[...]
        whole[rim + tokens :] = after[...]

    @pl.when(place[1] == 0)
    def _():
        values[:rim] = v_far[...]

    @pl.when(place[1] == CHIPS_APART - 1)
    def _():
        values[rim + tokens :] = v_far[...]

    acc_k[...] = jnp.zeros_like(acc_k)
    acc_v[...] = jnp.zeros_like(acc_v)
    blocks = 2 * band + 2
    odd = lax.broadcasted_iota(jnp.int32, (1, 2 * GRIDC), 1) >= GRIDC
    total = mask.shape[0]

    def block_bias(row, block):
        key_row = row - band + block
        inside = (key_row >= 0) & (key_row < total)
        sides = []
        for side in range(2):
            offset = block - side
            seen = inside & (mask[row + side, offset] == 1) if 0 <= offset <= 2 * band else False
            sides.append(jnp.where(seen, 0.0, MASKED).astype(jnp.float32))
        return jnp.where(odd, sides[1], sides[0])

    for pair in range(tokens // (2 * GRIDC)):
        here = pl.ds(pair * 2 * GRIDC, 2 * GRIDC)
        window = pl.ds(pair * 2 * GRIDC, blocks * GRIDC)

        def add_bias(scores):
            return jnp.concatenate(
                [
                    scores[b * GRIDC : (b + 1) * GRIDC] + block_bias(place[0] + 2 * pair, b)
                    for b in range(blocks)
                ],
                axis=0,
            )

        output, grad_query, grad_keys, grad_values = attend(
            q[here], d[here], keys[window], values[window], add_bias
        )
        out[here] = output
        dq[here] = grad_query
        acc_k[window] += grad_keys
        acc_v[window] += grad_values
    for acc, own, lo, hi, factor in ((acc_k, dk, lo_k, hi_k, SCALE), (acc_v, dv, lo_v, hi_v, 1.0)):
        own[...] = acc[rim : rim + tokens] * factor
        lo[...] = (acc[:rim] * factor).astype(lo.dtype)
        hi[...] = (acc[rim + tokens :] * factor).astype(hi.dtype)


def row_attention(place, mask, q, k, v, d, halos, band):
    tokens, feat = q.shape
    heads = feat // HEAD_DIM
    rim = band * GRIDC
    tall = pl.BlockSpec((tokens, HEAD_DIM), lambda h: (0, h))
    edge = pl.BlockSpec((rim, HEAD_DIM), lambda h: (0, h))
    scalars = pl.BlockSpec(memory_space=pltpu.SMEM)
    padded = tokens + 2 * rim
    pairs = tokens * (2 * band + 2) * GRIDC * heads
    return pl.pallas_call(
        functools.partial(row_kernel, band),
        grid=(heads,),
        in_specs=[scalars, scalars, tall, tall, tall, tall] + [edge] * 5,
        out_specs=[tall] * 4 + [edge] * 4,
        out_shape=[
            jax.ShapeDtypeStruct(q.shape, jnp.bfloat16),
            jax.ShapeDtypeStruct(q.shape, jnp.bfloat16),
            jax.ShapeDtypeStruct(q.shape, jnp.float32),
            jax.ShapeDtypeStruct(q.shape, jnp.float32),
        ]
        + [jax.ShapeDtypeStruct((rim, feat), jnp.bfloat16)] * 4,
        scratch_shapes=[
            pltpu.VMEM((padded, HEAD_DIM), jnp.bfloat16),
            pltpu.VMEM((padded, HEAD_DIM), jnp.bfloat16),
            pltpu.VMEM((padded, HEAD_DIM), jnp.float32),
            pltpu.VMEM((padded, HEAD_DIM), jnp.float32),
        ],
        compiler_params=pltpu.CompilerParams(vmem_limit_bytes=VMEM),
        cost_estimate=pl.CostEstimate(
            flops=240 * pairs * HEAD_DIM, bytes_accessed=30 * tokens * feat, transcendentals=pairs
        ),
        name="row_heads",
    )(place, mask, q, k, v, d, *halos)


def col_kernel(mask, x, earlier, out, bias):
    del earlier
    @pl.when((pl.program_id(0) == 0) & (pl.program_id(1) == 0))
    def _():
        size, total = bias.shape[0], mask.shape[0]
        row_of = lax.broadcasted_iota(jnp.int32, (size, total), 0) // GROUP
        spread = (row_of == lax.broadcasted_iota(jnp.int32, (size, total), 1)).astype(jnp.bfloat16)
        seen = (mask[...] == 1).astype(jnp.bfloat16)
        by_key = contract(spread, seen, 1, 1).astype(jnp.bfloat16)
        allowed = contract(by_key, spread, 1, 1)
        key_col = lax.broadcasted_iota(jnp.int32, (size, size), 0) % GROUP
        query_col = lax.broadcasted_iota(jnp.int32, (size, size), 1) % GROUP
        bias[...] = jnp.where((key_col == query_col) & (allowed > 0.5), 0.0, MASKED)

    shape = (x.shape[0], *x.shape[2:])
    tokens = shape[0] * shape[1] * shape[2]
    q, k, v, d = (x[:, a].reshape(tokens, HEAD_DIM) for a in range(4))
    chunk = min(tokens, 256)
    grad_keys, grad_values = 0.0, 0.0
    outputs, grads = [], []
    for start in range(0, tokens, chunk):
        here = slice(start, start + chunk)
        output, grad_query, more_keys, more_values = attend(
            q[here], d[here], k, v, lambda s: s + bias[:, here]
        )
        grad_keys += more_keys
        grad_values += more_values
        outputs.append(output)
        grads.append(grad_query)
    out[:, 0] = jnp.concatenate(outputs, 0).reshape(shape)
    out[:, 1] = jnp.concatenate(grads, 0).reshape(shape)
    out[:, 2] = (grad_keys * SCALE).astype(jnp.bfloat16).reshape(shape)
    out[:, 3] = grad_values.astype(jnp.bfloat16).reshape(shape)


def col_attention(mask, x, earlier, start, heads):
    n, k, rows, cols, _ = x.shape
    tokens = n * rows * GROUP
    block = (n, k, rows, GROUP, HEAD_DIM)
    pairs = tokens * tokens * heads * (cols // GROUP)
    return pl.pallas_call(
        col_kernel,
        grid=(heads, cols // GROUP),
        in_specs=[
            pl.BlockSpec(mask.shape, lambda h, g: (0, 0)),
            pl.BlockSpec(block, lambda h, g: (0, 0, 0, g, h + start)),
            pl.BlockSpec(memory_space=pl.ANY),
        ],
        out_specs=pl.BlockSpec(block, lambda h, g: (0, 0, 0, g, h)),
        out_shape=jax.ShapeDtypeStruct((n, k, rows, cols, heads * HEAD_DIM), jnp.bfloat16),
        scratch_shapes=[pltpu.VMEM((tokens, tokens), jnp.float32)],
        compiler_params=pltpu.CompilerParams(vmem_limit_bytes=VMEM),
        cost_estimate=pl.CostEstimate(
            flops=240 * pairs * HEAD_DIM, bytes_accessed=4 * x.size, transcendentals=pairs
        ),
        name="col_heads",
    )(mask, x, earlier)


def pack_kernel(*refs):
    *parts, out = refs
    for a, part in enumerate(parts):
        out[a] = part[...]


def packed(arrays, n):
    tokens, feat = arrays[0].shape
    rows, cols, k = tokens // GRIDC, GRIDC // n, len(arrays)
    return pl.pallas_call(
        pack_kernel,
        grid=(n,),
        in_specs=[pl.BlockSpec((rows, cols, feat), lambda j: (0, j, 0))] * k,
        out_specs=pl.BlockSpec((None, k, rows, cols, feat), lambda j: (j, 0, 0, 0, 0)),
        out_shape=jax.ShapeDtypeStruct((n, k, rows, cols, feat), jnp.bfloat16),
        compiler_params=pltpu.CompilerParams(vmem_limit_bytes=VMEM),
        cost_estimate=pl.CostEstimate(
            flops=0, bytes_accessed=4 * k * tokens * feat, transcendentals=0
        ),
        name="pack",
    )(*(a.reshape(rows, GRIDC, feat) for a in arrays))


def unpack_kernel(x, *refs):
    for a, part in enumerate(refs[-x.shape[0] :]):
        part[...] = x[a]


def unpacked(x, start, whole):
    n, k, rows, cols, width = x.shape
    kept = [] if isinstance(whole, int) else [a.reshape(rows, n * cols, -1) for a in whole]
    feat = kept[0].shape[-1] if kept else whole
    step = math.gcd(start, width) if start else width
    spec = pl.BlockSpec((rows, cols, step), lambda j, f: (0, j, start // step + f))
    outs = pl.pallas_call(
        unpack_kernel,
        grid=(n, width // step),
        in_specs=[pl.BlockSpec((None, k, rows, cols, step), lambda j, f: (j, 0, 0, 0, f))]
        + [pl.BlockSpec(memory_space=pl.ANY)] * len(kept),
        out_specs=[spec] * k,
        out_shape=[jax.ShapeDtypeStruct((rows, n * cols, feat), jnp.bfloat16)] * k,
        input_output_aliases={1 + a: a for a in range(len(kept))},
        compiler_params=pltpu.CompilerParams(vmem_limit_bytes=VMEM),
        cost_estimate=pl.CostEstimate(flops=0, bytes_accessed=4 * x.size, transcendentals=0),
        name="unpack",
    )(x, *kept)
    return [o.reshape(rows * n * cols, feat) for o in outs]


def swapped(lo_k, lo_v, hi_k, hi_v):
    n = lax.axis_size("ctx")
    up = [(i, i + 1) for i in range(n - 1)]
    down = [(j, i) for i, j in up]
    far = [(i, j) for i, j in up if j % CHIPS_APART == 0 and j + CHIPS_APART <= n]
    near_up = [pair for pair in up if pair not in far]
    near_down = [(j, i) for i, j in near_up]
    side = lax.axis_index("ctx") % CHIPS_APART
    first = [(i, i + CHIPS_APART) for i, _ in far] + [(j, j - CHIPS_APART) for _, j in far]
    second = [(i + CHIPS_APART, j) for i, j in far] + [(j - CHIPS_APART, i) for i, j in far]
    hop = lax.ppermute(jnp.where(side == 0, lo_v, hi_v), "ctx", first)
    k_before, k_after = lax.ppermute(hi_k, "ctx", up), lax.ppermute(lo_k, "ctx", down)
    v_before, v_after = lax.ppermute(hi_v, "ctx", near_up), lax.ppermute(lo_v, "ctx", near_down)
    far_v = lax.ppermute(hop, "ctx", second)
    return [k_before, v_before, k_after, v_after, far_v], hop


def exchanged(x):
    return lax.all_to_all(x, "ctx", 0, 0, tiled=True)


def body(
    row_query, row_key, row_value, row_cotangent, row_mask,
    col_query, col_key, col_value, col_cotangent, col_mask,
):
    n = lax.axis_size("ctx")
    tokens = row_query.shape[0]
    rows = tokens // GRIDC
    band = (row_mask.shape[1] - 1) // 2
    rim = band * GRIDC

    rims = [a for x in (row_key, row_value) for a in (x[:rim], x[tokens - rim :])]
    cols = [col_query, col_key, col_value, col_cotangent]
    *rims, cols = lax.optimization_barrier((*rims, cols))
    halos, hop = swapped(rims[0], rims[2], rims[1], rims[3])
    sent, hop = lax.optimization_barrier((packed(cols, n), hop))
    moved = exchanged(sent)

    me = lax.axis_index("ctx")
    place = jnp.stack([me * rows, me % CHIPS_APART])
    row_output, row_dquery, own_k, own_v, *sides = row_attention(
        place, row_mask, row_query, row_key, row_value, row_cotangent, halos, band
    )
    (k_before, v_before, k_after, v_after, far_v), hop = swapped(*sides)

    feat = col_query.shape[1]
    heads = feat // HEAD_DIM
    half = heads // 2
    first = col_attention(col_mask, moved, row_output, 0, half)
    first, k_before, k_after, hop = lax.optimization_barrier((first, k_before, k_after, hop))
    second = col_attention(col_mask, moved, first, half, heads - half)
    second, v_before, v_after, far_v = lax.optimization_barrier((second, v_before, v_after, far_v))
    first, second = exchanged(first), exchanged(second)
    col_results = unpacked(second, half * HEAD_DIM, unpacked(first, 0, feat))

    v_before = jnp.where(me % CHIPS_APART == 0, far_v, v_before)
    v_after = jnp.where(me % CHIPS_APART == CHIPS_APART - 1, far_v, v_after)
    row_grads = []
    for own, prev, following in ((own_k, k_before, k_after), (own_v, v_before, v_after)):
        gap = jnp.zeros((tokens - rim, own.shape[1]), own.dtype)
        added = jnp.concatenate([prev.astype(own.dtype), gap]) + jnp.concatenate(
            [gap, following.astype(own.dtype)]
        )
        row_grads.append((own + added).astype(jnp.bfloat16))
    return (
        row_output, row_dquery, *row_grads,
        *col_results,
    )


def solution(mesh):
    tokens, whole = P("ctx", "head"), P()
    return jax.shard_map(
        body,
        mesh=mesh,
        in_specs=(tokens,) * 4 + (whole,) + (tokens,) * 4 + (whole,),
        out_specs=(tokens,) * 8,
        check_vma=False,
    )
```

```python
import functools

import jax
import jax.numpy as jnp
import numpy as np
from jax import lax
from jax.experimental import pallas as pl
from jax.experimental.pallas import tpu as pltpu
from jax.sharding import PartitionSpec as P

HEAD_DIM = 128
GRIDC = 128
GROUP = 8
MASKED = -1e30
SCALE = HEAD_DIM**-0.5
EXP2_SCALE = SCALE * float(np.log2(np.e))
VMEM = 60 << 20
CHIPS_APART = 4


def contract(a, b, dim_a, dim_b):
    return lax.dot_general(
        a, b, (((dim_a,), (dim_b,)), ((), ())), preferred_element_type=jnp.float32
    )


def attend(queries, cotangent, keys, values, add_bias):
    n_keys, n_queries = keys.shape[0], queries.shape[0]
    scores = add_bias(contract(keys, queries, 1, 1))
    top = jnp.max(scores, axis=0, keepdims=True)
    terms = jnp.exp2((scores - top) * EXP2_SCALE)
    prob = terms * (1.0 / jnp.sum(terms, axis=0, keepdims=True))
    prob_low = prob.astype(jnp.bfloat16)
    output = contract(prob_low, values, 0, 0).astype(jnp.bfloat16)
    product = cotangent.astype(jnp.float32) * output.astype(jnp.float32)
    delta = jnp.sum(product.T, axis=0, keepdims=True)
    d_prob = contract(values, cotangent, 1, 1)
    d_scores = (prob * (d_prob - delta)).astype(jnp.bfloat16)
    grad_query = (contract(d_scores, keys, 0, 0) * SCALE).astype(jnp.bfloat16)
    grad_keys = contract(d_scores, queries, 1, 0)
    grad_values = contract(prob_low, cotangent, 1, 0)
    return output, grad_query, grad_keys, grad_values


def row_kernel(
    band, place, mask, q, k, v, d, k_lo, v_lo, k_hi, v_hi, v_far,
    out, dq, dk, dv, lo_k, lo_v, hi_k, hi_v, keys, values, acc_k, acc_v,
):
    tokens = q.shape[0]
    rim = k_lo.shape[0]
    for whole, before, own, after in ((keys, k_lo, k, k_hi), (values, v_lo, v, v_hi)):
        whole[:rim] = before[...]
        whole[rim : rim + tokens] = own[...]
        whole[rim + tokens :] = after[...]

    @pl.when(place[1] == 0)
    def _():
        values[:rim] = v_far[...]

    @pl.when(place[1] == CHIPS_APART - 1)
    def _():
        values[rim + tokens :] = v_far[...]

    acc_k[...] = jnp.zeros_like(acc_k)
    acc_v[...] = jnp.zeros_like(acc_v)
    blocks = 2 * band + 2
    odd = lax.broadcasted_iota(jnp.int32, (1, 2 * GRIDC), 1) >= GRIDC
    total = mask.shape[0]

    def block_bias(row, block):
        key_row = row - band + block
        inside = (key_row >= 0) & (key_row < total)
        sides = []
        for side in range(2):
            offset = block - side
            seen = inside & (mask[row + side, offset] == 1) if 0 <= offset <= 2 * band else False
            sides.append(jnp.where(seen, 0.0, MASKED).astype(jnp.float32))
        return jnp.where(odd, sides[1], sides[0])

    for pair in range(tokens // (2 * GRIDC)):
        here = pl.ds(pair * 2 * GRIDC, 2 * GRIDC)
        window = pl.ds(pair * 2 * GRIDC, blocks * GRIDC)

        def add_bias(scores):
            return jnp.concatenate(
                [
                    scores[b * GRIDC : (b + 1) * GRIDC] + block_bias(place[0] + 2 * pair, b)
                    for b in range(blocks)
                ],
                axis=0,
            )

        output, grad_query, grad_keys, grad_values = attend(
            q[here], d[here], keys[window], values[window], add_bias
        )
        out[here] = output
        dq[here] = grad_query
        acc_k[window] += grad_keys
        acc_v[window] += grad_values
    for acc, own, lo, hi, factor in ((acc_k, dk, lo_k, hi_k, SCALE), (acc_v, dv, lo_v, hi_v, 1.0)):
        own[...] = acc[rim : rim + tokens] * factor
        lo[...] = (acc[:rim] * factor).astype(lo.dtype)
        hi[...] = (acc[rim + tokens :] * factor).astype(hi.dtype)


def row_attention(place, mask, q, k, v, d, halos, band):
    tokens, feat = q.shape
    heads = feat // HEAD_DIM
    rim = band * GRIDC
    tall = pl.BlockSpec((tokens, HEAD_DIM), lambda h: (0, h))
    edge = pl.BlockSpec((rim, HEAD_DIM), lambda h: (0, h))
    scalars = pl.BlockSpec(memory_space=pltpu.SMEM)
    padded = tokens + 2 * rim
    pairs = tokens * (2 * band + 2) * GRIDC * heads
    return pl.pallas_call(
        functools.partial(row_kernel, band),
        grid=(heads,),
        in_specs=[scalars, scalars, tall, tall, tall, tall] + [edge] * 5,
        out_specs=[tall] * 4 + [edge] * 4,
        out_shape=[
            jax.ShapeDtypeStruct(q.shape, jnp.bfloat16),
            jax.ShapeDtypeStruct(q.shape, jnp.bfloat16),
            jax.ShapeDtypeStruct(q.shape, jnp.float32),
            jax.ShapeDtypeStruct(q.shape, jnp.float32),
        ]
        + [jax.ShapeDtypeStruct((rim, feat), jnp.bfloat16)] * 4,
        scratch_shapes=[
            pltpu.VMEM((padded, HEAD_DIM), jnp.bfloat16),
            pltpu.VMEM((padded, HEAD_DIM), jnp.bfloat16),
            pltpu.VMEM((padded, HEAD_DIM), jnp.float32),
            pltpu.VMEM((padded, HEAD_DIM), jnp.float32),
        ],
        compiler_params=pltpu.CompilerParams(vmem_limit_bytes=VMEM),
        cost_estimate=pl.CostEstimate(
            flops=240 * pairs * HEAD_DIM, bytes_accessed=30 * tokens * feat, transcendentals=pairs
        ),
        name="row_heads",
    )(place, mask, q, k, v, d, *halos)


def col_kernel(me, mask, x, earlier, *refs):
    *outs, result, bias = refs
    del earlier

    @pl.when((pl.program_id(0) == 0) & (pl.program_id(1) == 0))
    def _():
        size, total = bias.shape[0], mask.shape[0]
        row_of = lax.broadcasted_iota(jnp.int32, (size, total), 0) // GROUP
        spread = (row_of == lax.broadcasted_iota(jnp.int32, (size, total), 1)).astype(jnp.bfloat16)
        seen = (mask[...] == 1).astype(jnp.bfloat16)
        by_key = contract(spread, seen, 1, 1).astype(jnp.bfloat16)
        allowed = contract(by_key, spread, 1, 1)
        key_col = lax.broadcasted_iota(jnp.int32, (size, size), 0) % GROUP
        query_col = lax.broadcasted_iota(jnp.int32, (size, size), 1) % GROUP
        bias[...] = jnp.where((key_col == query_col) & (allowed > 0.5), 0.0, MASKED)

    shape = (x.shape[0], *x.shape[2:])
    tokens = shape[0] * shape[1] * shape[2]
    q, k, v, d = (x[:, a].reshape(tokens, HEAD_DIM) for a in range(4))
    chunk = min(tokens, 256)
    grad_keys, grad_values = 0.0, 0.0
    outputs, grads = [], []
    for start in range(0, tokens, chunk):
        here = slice(start, start + chunk)
        output, grad_query, more_keys, more_values = attend(
            q[here], d[here], k, v, lambda s: s + bias[:, here]
        )
        grad_keys += more_keys
        grad_values += more_values
        outputs.append(output)
        grads.append(grad_query)
    result[:, 0] = jnp.concatenate(outputs, 0).reshape(shape)
    result[:, 1] = jnp.concatenate(grads, 0).reshape(shape)
    result[:, 2] = (grad_keys * SCALE).astype(jnp.bfloat16).reshape(shape)
    result[:, 3] = grad_values.astype(jnp.bfloat16).reshape(shape)
    for partner, out in enumerate(outs):
        out[...] = result[me[0] ^ partner]


def col_attention(me, mask, x, earlier):
    n, k, rows, cols, feat = x.shape
    heads = feat // HEAD_DIM
    tokens = n * rows * GROUP
    block = (k, rows, GROUP, HEAD_DIM)
    pairs = tokens * tokens * heads * (cols // GROUP)
    return pl.pallas_call(
        col_kernel,
        grid=(heads, cols // GROUP),
        in_specs=[
            pl.BlockSpec(memory_space=pltpu.SMEM),
            pl.BlockSpec(mask.shape, lambda h, g: (0, 0)),
            pl.BlockSpec((n, *block), lambda h, g: (0, 0, 0, g, h)),
            pl.BlockSpec(memory_space=pl.ANY),
        ],
        out_specs=[pl.BlockSpec(block, lambda h, g: (0, 0, g, h))] * n,
        out_shape=[jax.ShapeDtypeStruct((k, rows, cols, feat), jnp.bfloat16)] * n,
        scratch_shapes=[
            pltpu.VMEM((n, *block), jnp.bfloat16),
            pltpu.VMEM((tokens, tokens), jnp.float32),
        ],
        compiler_params=pltpu.CompilerParams(vmem_limit_bytes=VMEM),
        cost_estimate=pl.CostEstimate(
            flops=240 * pairs * HEAD_DIM, bytes_accessed=4 * x.size, transcendentals=pairs
        ),
        name="col_heads",
    )(me, mask, x, earlier)


def pack_kernel(n, *refs):
    *parts, out, held, arrived, left = refs
    cols = GRIDC // n
    loads = [
        pltpu.make_async_copy(part, held.at[a], arrived.at[a]) for a, part in enumerate(parts)
    ]
    stores = [
        [
            pltpu.make_async_copy(
                held.at[a, :, j * cols : (j + 1) * cols, :], out.at[j, a], left.at[a, j]
            )
            for j in range(n)
        ]
        for a in range(len(parts))
    ]
    for load in loads:
        load.start()
    for load, several in zip(loads, stores):
        load.wait()
        for store in several:
            store.start()
    for several in stores:
        for store in several:
            store.wait()


def packed(arrays, n):
    tokens, feat = arrays[0].shape
    rows, cols, k = tokens // GRIDC, GRIDC // n, len(arrays)
    return pl.pallas_call(
        functools.partial(pack_kernel, n),
        in_specs=[pl.BlockSpec(memory_space=pl.ANY)] * k,
        out_specs=pl.BlockSpec(memory_space=pl.ANY),
        out_shape=jax.ShapeDtypeStruct((n, k, rows, cols, feat), jnp.bfloat16),
        scratch_shapes=[
            pltpu.VMEM((k, rows, GRIDC, feat), jnp.bfloat16),
            pltpu.SemaphoreType.DMA((k,)),
            pltpu.SemaphoreType.DMA((k, n)),
        ],
        compiler_params=pltpu.CompilerParams(vmem_limit_bytes=VMEM),
        cost_estimate=pl.CostEstimate(
            flops=0, bytes_accessed=4 * k * tokens * feat, transcendentals=0
        ),
        name="pack",
    )(*(a.reshape(rows, GRIDC, feat) for a in arrays))


def unpack_kernel(n, me, *refs):
    parts, outs, (held, arrived, left) = refs[:n], refs[n:-3], refs[-3:]
    cols = GRIDC // n
    loads, stores = [], []
    for a, out in enumerate(outs):
        for partner, part in enumerate(parts):
            here = pl.ds(pl.multiple_of((me[0] ^ partner) * cols, cols), cols)
            loads.append(
                pltpu.make_async_copy(
                    part.at[a], held.at[a, :, here, :], arrived.at[a, partner]
                )
            )
        stores.append(pltpu.make_async_copy(held.at[a], out, left.at[a]))
    for load in loads:
        load.start()
    for a, store in enumerate(stores):
        for load in loads[a * n : (a + 1) * n]:
            load.wait()
        store.start()
    for store in stores:
        store.wait()


def unpacked(me, parts):
    n = len(parts)
    k, rows, cols, feat = parts[0].shape
    outs = pl.pallas_call(
        functools.partial(unpack_kernel, n),
        in_specs=[pl.BlockSpec(memory_space=pltpu.SMEM)] + [pl.BlockSpec(memory_space=pl.ANY)] * n,
        out_specs=[pl.BlockSpec(memory_space=pl.ANY)] * k,
        out_shape=[jax.ShapeDtypeStruct((rows, GRIDC, feat), jnp.bfloat16)] * k,
        scratch_shapes=[
            pltpu.VMEM((k, rows, GRIDC, feat), jnp.bfloat16),
            pltpu.SemaphoreType.DMA((k, n)),
            pltpu.SemaphoreType.DMA((k,)),
        ],
        compiler_params=pltpu.CompilerParams(vmem_limit_bytes=VMEM),
        cost_estimate=pl.CostEstimate(
            flops=0, bytes_accessed=4 * k * rows * GRIDC * feat, transcendentals=0
        ),
        name="unpack",
    )(me, *parts)
    return [o.reshape(rows * GRIDC, feat) for o in outs]


def swapped(lo_k, lo_v, hi_k, hi_v):
    n = lax.axis_size("ctx")
    up = [(i, i + 1) for i in range(n - 1)]
    down = [(j, i) for i, j in up]
    far = [(i, j) for i, j in up if j % CHIPS_APART == 0 and j + CHIPS_APART <= n]
    near_up = [pair for pair in up if pair not in far]
    near_down = [(j, i) for i, j in near_up]
    side = lax.axis_index("ctx") % CHIPS_APART
    first = [(i, i + CHIPS_APART) for i, _ in far] + [(j, j - CHIPS_APART) for _, j in far]
    second = [(i + CHIPS_APART, j) for i, j in far] + [(j - CHIPS_APART, i) for i, j in far]
    hop = lax.ppermute(jnp.where(side == 0, lo_v, hi_v), "ctx", first)
    k_before, k_after = lax.ppermute(hi_k, "ctx", up), lax.ppermute(lo_k, "ctx", down)
    v_before, v_after = lax.ppermute(hi_v, "ctx", near_up), lax.ppermute(lo_v, "ctx", near_down)
    far_v = lax.ppermute(hop, "ctx", second)
    return [k_before, v_before, k_after, v_after, far_v], hop


def exchanged(x):
    return lax.all_to_all(x, "ctx", 0, 0, tiled=True)


def body(
    row_query, row_key, row_value, row_cotangent, row_mask,
    col_query, col_key, col_value, col_cotangent, col_mask,
):
    n = lax.axis_size("ctx")
    tokens = row_query.shape[0]
    rows = tokens // GRIDC
    band = (row_mask.shape[1] - 1) // 2
    rim = band * GRIDC

    rims = [a for x in (row_key, row_value) for a in (x[:rim], x[tokens - rim :])]
    cols = [col_query, col_key, col_value, col_cotangent]
    *rims, cols = lax.optimization_barrier((*rims, cols))
    halos, hop = swapped(rims[0], rims[2], rims[1], rims[3])
    sent, hop = lax.optimization_barrier((packed(cols, n), hop))
    moved = exchanged(sent)

    me = lax.axis_index("ctx")
    place = jnp.stack([me * rows, me % CHIPS_APART])
    row_output, row_dquery, own_k, own_v, *sides = row_attention(
        place, row_mask, row_query, row_key, row_value, row_cotangent, halos, band
    )
    halos, _ = swapped(*sides)

    results = col_attention(me.reshape(1), col_mask, moved, row_output)
    results, halos = lax.optimization_barrier((results, halos))
    returned = [results[0]] + [
        lax.ppermute(results[k], "ctx", [(i, i ^ k) for i in range(n)]) for k in range(1, n)
    ]
    col_results = unpacked(me.reshape(1), returned)

    k_before, v_before, k_after, v_after, far_v = halos
    v_before = jnp.where(me % CHIPS_APART == 0, far_v, v_before)
    v_after = jnp.where(me % CHIPS_APART == CHIPS_APART - 1, far_v, v_after)
    row_grads = []
    for own, prev, following in ((own_k, k_before, k_after), (own_v, v_before, v_after)):
        gap = jnp.zeros((tokens - rim, own.shape[1]), own.dtype)
        added = jnp.concatenate([prev.astype(own.dtype), gap]) + jnp.concatenate(
            [gap, following.astype(own.dtype)]
        )
        row_grads.append((own + added).astype(jnp.bfloat16))
    return (
        row_output, row_dquery, *row_grads,
        *col_results,
    )


def solution(mesh):
    tokens, whole = P("ctx", "head"), P()
    return jax.shard_map(
        body,
        mesh=mesh,
        in_specs=(tokens,) * 4 + (whole,) + (tokens,) * 4 + (whole,),
        out_specs=(tokens,) * 8,
        check_vma=False,
    )
```

```python
import functools

import jax
import jax.numpy as jnp
import numpy as np
from jax import lax
from jax.experimental import pallas as pl
from jax.experimental.pallas import tpu as pltpu
from jax.sharding import PartitionSpec as P

HEAD_DIM = 128
GRIDC = 128
GROUP = 8
MASKED = -1e30
SCALE = HEAD_DIM**-0.5
EXP2_SCALE = SCALE * float(np.log2(np.e))
VMEM = 60 << 20
CHIPS_APART = 4


def contract(a, b, dim_a, dim_b):
    return lax.dot_general(
        a, b, (((dim_a,), (dim_b,)), ((), ())), preferred_element_type=jnp.float32
    )


def attend(queries, cotangent, keys, values, add_bias):
    n_keys, n_queries = keys.shape[0], queries.shape[0]
    scores = add_bias(contract(keys, queries, 1, 1))
    top = jnp.max(scores, axis=0, keepdims=True)
    terms = jnp.exp2((scores - top) * EXP2_SCALE)
    prob = terms * (1.0 / jnp.sum(terms, axis=0, keepdims=True))
    prob_low = prob.astype(jnp.bfloat16)
    output = contract(prob_low, values, 0, 0).astype(jnp.bfloat16)
    product = cotangent.astype(jnp.float32) * output.astype(jnp.float32)
    delta = jnp.sum(product.T, axis=0, keepdims=True)
    d_prob = contract(values, cotangent, 1, 1)
    d_scores = (prob * (d_prob - delta)).astype(jnp.bfloat16)
    grad_query = (contract(d_scores, keys, 0, 0) * SCALE).astype(jnp.bfloat16)
    grad_keys = contract(d_scores, queries, 1, 0)
    grad_values = contract(prob_low, cotangent, 1, 0)
    return output, grad_query, grad_keys, grad_values


def row_kernel(
    band, place, mask, q, k, v, d, inner_kv, outer_k, outer_v, far_v,
    out, dq, dk, dv, inner_grads, outer_dk, outer_dv, keys, values, acc_k, acc_v,
):
    tokens = q.shape[0]
    rim = outer_k.shape[0]
    odd_device = place[1]
    inner = pl.ds(pl.multiple_of((1 - odd_device) * (rim + tokens), GRIDC), rim)
    outer = pl.ds(pl.multiple_of(odd_device * (rim + tokens), GRIDC), rim)
    keys[rim : rim + tokens] = k[...]
    values[rim : rim + tokens] = v[...]
    keys[inner] = inner_kv[0]
    values[inner] = inner_kv[1]
    keys[outer] = outer_k[...]

    @pl.when(place[2] == 0)
    def _():
        values[outer] = outer_v[...]

    @pl.when(place[2] == 1)
    def _():
        values[outer] = far_v[...]

    acc_k[...] = jnp.zeros_like(acc_k)
    acc_v[...] = jnp.zeros_like(acc_v)
    blocks = 2 * band + 2
    odd = lax.broadcasted_iota(jnp.int32, (1, 2 * GRIDC), 1) >= GRIDC
    total = mask.shape[0]

    def block_bias(row, block):
        key_row = row - band + block
        inside = (key_row >= 0) & (key_row < total)
        sides = []
        for side in range(2):
            offset = block - side
            seen = inside & (mask[row + side, offset] == 1) if 0 <= offset <= 2 * band else False
            sides.append(jnp.where(seen, 0.0, MASKED).astype(jnp.float32))
        return jnp.where(odd, sides[1], sides[0])

    for pair in range(tokens // (2 * GRIDC)):
        here = pl.ds(pair * 2 * GRIDC, 2 * GRIDC)
        window = pl.ds(pair * 2 * GRIDC, blocks * GRIDC)

        def add_bias(scores):
            return jnp.concatenate(
                [
                    scores[b * GRIDC : (b + 1) * GRIDC] + block_bias(place[0] + 2 * pair, b)
                    for b in range(blocks)
                ],
                axis=0,
            )

        output, grad_query, grad_keys, grad_values = attend(
            q[here], d[here], keys[window], values[window], add_bias
        )
        out[here] = output
        dq[here] = grad_query
        acc_k[window] += grad_keys
        acc_v[window] += grad_values
    sides = ((acc_k, dk, outer_dk, SCALE), (acc_v, dv, outer_dv, 1.0))
    for at, (acc, own, across, factor) in enumerate(sides):
        own[...] = acc[rim : rim + tokens] * factor
        inner_grads[at] = (acc[inner] * factor).astype(across.dtype)
        across[...] = (acc[outer] * factor).astype(across.dtype)


def row_attention(place, mask, q, k, v, d, halos, band):
    tokens, feat = q.shape
    heads = feat // HEAD_DIM
    rim = band * GRIDC
    tall = pl.BlockSpec((tokens, HEAD_DIM), lambda h: (0, h))
    edge = pl.BlockSpec((rim, HEAD_DIM), lambda h: (0, h))
    both = pl.BlockSpec((2, rim, HEAD_DIM), lambda h: (0, 0, h))
    scalars = pl.BlockSpec(memory_space=pltpu.SMEM)
    padded = tokens + 2 * rim
    pairs = tokens * (2 * band + 2) * GRIDC * heads
    return pl.pallas_call(
        functools.partial(row_kernel, band),
        grid=(heads,),
        in_specs=[scalars, scalars, tall, tall, tall, tall, both, edge, edge, edge],
        out_specs=[tall] * 4 + [both, edge, edge],
        out_shape=[
            jax.ShapeDtypeStruct(q.shape, jnp.bfloat16),
            jax.ShapeDtypeStruct(q.shape, jnp.bfloat16),
            jax.ShapeDtypeStruct(q.shape, jnp.float32),
            jax.ShapeDtypeStruct(q.shape, jnp.float32),
            jax.ShapeDtypeStruct((2, rim, feat), jnp.bfloat16),
            jax.ShapeDtypeStruct((rim, feat), jnp.bfloat16),
            jax.ShapeDtypeStruct((rim, feat), jnp.bfloat16),
        ],
        scratch_shapes=[
            pltpu.VMEM((padded, HEAD_DIM), jnp.bfloat16),
            pltpu.VMEM((padded, HEAD_DIM), jnp.bfloat16),
            pltpu.VMEM((padded, HEAD_DIM), jnp.float32),
            pltpu.VMEM((padded, HEAD_DIM), jnp.float32),
        ],
        compiler_params=pltpu.CompilerParams(vmem_limit_bytes=VMEM),
        cost_estimate=pl.CostEstimate(
            flops=240 * pairs * HEAD_DIM, bytes_accessed=30 * tokens * feat, transcendentals=pairs
        ),
        name="row_heads",
    )(place, mask, q, k, v, d, *halos)


def col_kernel(n_parts, me, mask, x, earlier, *refs):
    outs, result, bias = refs[:n_parts], refs[n_parts], refs[-1]
    del earlier

    @pl.when((pl.program_id(0) == 0) & (pl.program_id(1) == 0))
    def _():
        size, total = bias.shape[0], mask.shape[0]
        row_of = lax.broadcasted_iota(jnp.int32, (size, total), 0) // GROUP
        spread = (row_of == lax.broadcasted_iota(jnp.int32, (size, total), 1)).astype(jnp.bfloat16)
        seen = (mask[...] == 1).astype(jnp.bfloat16)
        by_key = contract(spread, seen, 1, 1).astype(jnp.bfloat16)
        allowed = contract(by_key, spread, 1, 1)
        key_col = lax.broadcasted_iota(jnp.int32, (size, size), 0) % GROUP
        query_col = lax.broadcasted_iota(jnp.int32, (size, size), 1) % GROUP
        bias[...] = jnp.where((key_col == query_col) & (allowed > 0.5), 0.0, MASKED)

    shape = (x.shape[0], *x.shape[2:])
    tokens = shape[0] * shape[1] * shape[2]
    q, k, v, d = (x[:, a].reshape(tokens, HEAD_DIM) for a in range(4))
    chunk = min(tokens, 256)
    grad_keys, grad_values = 0.0, 0.0
    outputs, grads = [], []
    for start in range(0, tokens, chunk):
        here = slice(start, start + chunk)
        output, grad_query, more_keys, more_values = attend(
            q[here], d[here], k, v, lambda s: s + bias[:, here]
        )
        grad_keys += more_keys
        grad_values += more_values
        outputs.append(output)
        grads.append(grad_query)
    result[:, 0] = jnp.concatenate(outputs, 0).reshape(shape)
    result[:, 1] = jnp.concatenate(grads, 0).reshape(shape)
    result[:, 2] = (grad_keys * SCALE).astype(jnp.bfloat16).reshape(shape)
    result[:, 3] = grad_values.astype(jnp.bfloat16).reshape(shape)
    for partner, out in enumerate(outs):
        out[...] = result[me[0] ^ partner]


def col_attention(me, mask, x, earlier, start, heads, in_parts):
    n, k, rows, cols, _ = x.shape
    n_parts = n if in_parts else 0
    tokens = n * rows * GROUP
    block = (k, rows, GROUP, HEAD_DIM)
    pairs = tokens * tokens * heads * (cols // GROUP)
    part = (k, rows, cols, heads * HEAD_DIM)
    if in_parts:
        out_specs = [pl.BlockSpec(block, lambda h, g: (0, 0, g, h))] * n
        out_shape = [jax.ShapeDtypeStruct(part, jnp.bfloat16)] * n
        held = [pltpu.VMEM((n, *block), jnp.bfloat16)]
    else:
        out_specs = pl.BlockSpec((n, *block), lambda h, g: (0, 0, 0, g, h))
        out_shape = jax.ShapeDtypeStruct((n, *part), jnp.bfloat16)
        held = []
    return pl.pallas_call(
        functools.partial(col_kernel, n_parts),
        grid=(heads, cols // GROUP),
        in_specs=[
            pl.BlockSpec(memory_space=pltpu.SMEM),
            pl.BlockSpec(mask.shape, lambda h, g: (0, 0)),
            pl.BlockSpec((n, *block), lambda h, g: (0, 0, 0, g, h + start)),
            pl.BlockSpec(memory_space=pl.ANY),
        ],
        out_specs=out_specs,
        out_shape=out_shape,
        scratch_shapes=held + [pltpu.VMEM((tokens, tokens), jnp.float32)],
        compiler_params=pltpu.CompilerParams(vmem_limit_bytes=VMEM),
        cost_estimate=pl.CostEstimate(
            flops=240 * pairs * HEAD_DIM, bytes_accessed=4 * x.size, transcendentals=pairs
        ),
        name="col_heads",
    )(me, mask, x, earlier)


def pack_kernel(n, *refs):
    *parts, out, held, arrived, left = refs
    cols = GRIDC // n
    loads = [
        pltpu.make_async_copy(part, held.at[a], arrived.at[a]) for a, part in enumerate(parts)
    ]
    stores = [
        [
            pltpu.make_async_copy(
                held.at[a, :, j * cols : (j + 1) * cols, :], out.at[j, a], left.at[a, j]
            )
            for j in range(n)
        ]
        for a in range(len(parts))
    ]
    for load in loads:
        load.start()
    for load, several in zip(loads, stores):
        load.wait()
        for store in several:
            store.start()
    for several in stores:
        for store in several:
            store.wait()


def packed(arrays, n):
    tokens, feat = arrays[0].shape
    rows, cols, k = tokens // GRIDC, GRIDC // n, len(arrays)
    return pl.pallas_call(
        functools.partial(pack_kernel, n),
        in_specs=[pl.BlockSpec(memory_space=pl.ANY)] * k,
        out_specs=pl.BlockSpec(memory_space=pl.ANY),
        out_shape=jax.ShapeDtypeStruct((n, k, rows, cols, feat), jnp.bfloat16),
        scratch_shapes=[
            pltpu.VMEM((k, rows, GRIDC, feat), jnp.bfloat16),
            pltpu.SemaphoreType.DMA((k,)),
            pltpu.SemaphoreType.DMA((k, n)),
        ],
        compiler_params=pltpu.CompilerParams(vmem_limit_bytes=VMEM),
        cost_estimate=pl.CostEstimate(
            flops=0, bytes_accessed=4 * k * tokens * feat, transcendentals=0
        ),
        name="pack",
    )(*(a.reshape(rows, GRIDC, feat) for a in arrays))


def unpack_kernel(in_parts, n, start, me, *refs):
    held, arrived, left = refs[-3:]
    k, _, _, width = held.shape
    outs = refs[-3 - k : -3]
    cols = GRIDC // n
    loads, stores = [], []
    for a, out in enumerate(outs):
        for i in range(n):
            if in_parts:
                part, source = refs[i], me[0] ^ i
            else:
                part, source = refs[0].at[i], i
            here = pl.ds(pl.multiple_of(source * cols, cols), cols)
            loads.append(
                pltpu.make_async_copy(part.at[a], held.at[a, :, here, :], arrived.at[a, i])
            )
        stores.append(
            pltpu.make_async_copy(held.at[a], out.at[:, :, start : start + width], left.at[a])
        )
    for load in loads:
        load.start()
    for a, store in enumerate(stores):
        for load in loads[a * n : (a + 1) * n]:
            load.wait()
        store.start()
    for store in stores:
        store.wait()


def unpacked(me, parts, start, feat, kept):
    in_parts = isinstance(parts, list)
    parts = parts if in_parts else [parts]
    k, rows, cols, width = parts[0].shape[-4:]
    n = GRIDC // cols
    kept = [a.reshape(rows, GRIDC, feat) for a in kept]
    outs = pl.pallas_call(
        functools.partial(unpack_kernel, in_parts, n, start),
        in_specs=[pl.BlockSpec(memory_space=pltpu.SMEM)]
        + [pl.BlockSpec(memory_space=pl.ANY)] * (len(parts) + len(kept)),
        out_specs=[pl.BlockSpec(memory_space=pl.ANY)] * k,
        out_shape=[jax.ShapeDtypeStruct((rows, GRIDC, feat), jnp.bfloat16)] * k,
        scratch_shapes=[
            pltpu.VMEM((k, rows, GRIDC, width), jnp.bfloat16),
            pltpu.SemaphoreType.DMA((k, n)),
            pltpu.SemaphoreType.DMA((k,)),
        ],
        input_output_aliases={1 + len(parts) + a: a for a in range(len(kept))},
        compiler_params=pltpu.CompilerParams(vmem_limit_bytes=VMEM),
        cost_estimate=pl.CostEstimate(
            flops=0, bytes_accessed=4 * k * rows * GRIDC * width, transcendentals=0
        ),
        name="unpack",
    )(me, *parts, *kept)
    return [o.reshape(rows * GRIDC, feat) for o in outs]


def swapped(inner, outer_k, outer_v):
    n = lax.axis_size("ctx")
    across = [(i, i + 1) for i in range(1, n - 1, 2)]
    far = [(i, j) for i, j in across if j % CHIPS_APART == 0 and j + CHIPS_APART <= n]
    near = [pair for pair in across if pair not in far]
    back = lambda pairs: [(j, i) for i, j in pairs]
    step = CHIPS_APART
    first = [(i, i + step) for i, _ in far] + [(j, j - step) for _, j in far]
    second = [(i + step, j) for i, j in far] + [(j - step, i) for i, j in far]
    outer_v = lax.ppermute(outer_v, "ctx", near + back(near) + first)
    outer_k = lax.ppermute(outer_k, "ctx", across + back(across))
    inner = lax.ppermute(inner, "ctx", [(i, i ^ 1) for i in range(n)])
    far_v = lax.ppermute(outer_v, "ctx", second)
    return inner, outer_k, outer_v, far_v


def exchanged(x):
    return lax.all_to_all(x, "ctx", 0, 0, tiled=True)


def body(
    row_query, row_key, row_value, row_cotangent, row_mask,
    col_query, col_key, col_value, col_cotangent, col_mask,
):
    n = lax.axis_size("ctx")
    tokens = row_query.shape[0]
    rows = tokens // GRIDC
    band = (row_mask.shape[1] - 1) // 2
    rim = band * GRIDC

    feat = row_key.shape[1]
    me = lax.axis_index("ctx")
    odd = me % 2
    side = me % CHIPS_APART
    inner_at, outer_at = (1 - odd) * (tokens - rim), odd * (tokens - rim)
    rim_of = lambda x, at: lax.dynamic_slice_in_dim(x, at, rim, 0)
    inner = jnp.stack([rim_of(row_key, inner_at), rim_of(row_value, inner_at)])
    outer_k, outer_v = rim_of(row_key, outer_at), rim_of(row_value, outer_at)
    cols = [col_query, col_key, col_value, col_cotangent]
    inner, outer_k, outer_v, cols = lax.optimization_barrier((inner, outer_k, outer_v, cols))
    halos = swapped(inner, outer_k, outer_v)
    sent, outer_v = lax.optimization_barrier((packed(cols, n), halos[2]))
    moved = exchanged(sent)

    is_far = (side == 0) | (side == CHIPS_APART - 1)
    place = jnp.stack([me * rows, odd, is_far.astype(odd.dtype)])
    row_output, row_dquery, own_k, own_v, *sides = row_attention(
        place, row_mask, row_query, row_key, row_value, row_cotangent, halos, band
    )
    inner, outer_k, outer_v, far_v = swapped(*sides)

    heads = col_query.shape[1] // HEAD_DIM
    half = heads // 2
    where = me.reshape(1)
    partners = [[(i, i ^ k) for i in range(n)] for k in range(n)]
    send = lambda parts: [parts[0]] + [
        lax.ppermute(part, "ctx", pairs) for part, pairs in zip(parts[1:], partners[1:])
    ]
    first = col_attention(where, col_mask, moved, row_output, 0, half, False)
    first, inner, outer_k, outer_v = lax.optimization_barrier((first, inner, outer_k, outer_v))
    second = col_attention(where, col_mask, moved, first, half, heads - half, True)
    second, far_v = lax.optimization_barrier((second, far_v))
    first, second = exchanged(first), send(second)
    col_feat = col_query.shape[1]
    col_results = unpacked(where, first, 0, col_feat, [])
    col_results = unpacked(where, second, half * HEAD_DIM, col_feat, col_results)

    outer_v = jnp.where(is_far, far_v, outer_v)
    row_grads = []
    for own, near, across in ((own_k, inner[0], outer_k), (own_v, inner[1], outer_v)):
        lo = jnp.where(odd == 1, near, across).astype(own.dtype)
        hi = jnp.where(odd == 1, across, near).astype(own.dtype)
        gap = jnp.zeros((tokens - rim, feat), own.dtype)
        added = jnp.concatenate([lo, gap]) + jnp.concatenate([gap, hi])
        row_grads.append((own + added).astype(jnp.bfloat16))
    return (
        row_output, row_dquery, *row_grads,
        *col_results,
    )


def solution(mesh):
    tokens, whole = P("ctx", "head"), P()
    return jax.shard_map(
        body,
        mesh=mesh,
        in_specs=(tokens,) * 4 + (whole,) + (tokens,) * 4 + (whole,),
        out_specs=(tokens,) * 8,
        check_vma=False,
    )
```

```python
import functools

import jax
import jax.numpy as jnp
import numpy as np
from jax import lax
from jax.experimental import pallas as pl
from jax.experimental.pallas import tpu as pltpu
from jax.sharding import PartitionSpec as P

HEAD_DIM = 128
GRIDC = 128
GROUP = 8
MASKED = -1e30
SCALE = HEAD_DIM**-0.5
EXP2_SCALE = SCALE * float(np.log2(np.e))
VMEM = 60 << 20
CHIPS_APART = 4


def contract(a, b, dim_a, dim_b):
    return lax.dot_general(
        a, b, (((dim_a,), (dim_b,)), ((), ())), preferred_element_type=jnp.float32
    )


def attend(queries, cotangent, keys, values, add_bias):
    n_keys, n_queries = keys.shape[0], queries.shape[0]
    scores = add_bias(contract(keys, queries, 1, 1))
    top = jnp.max(scores, axis=0, keepdims=True)
    terms = jnp.exp2((scores - top) * EXP2_SCALE)
    prob = terms * (1.0 / jnp.sum(terms, axis=0, keepdims=True))
    prob_low = prob.astype(jnp.bfloat16)
    output = contract(prob_low, values, 0, 0).astype(jnp.bfloat16)
    product = cotangent.astype(jnp.float32) * output.astype(jnp.float32)
    delta = jnp.sum(product.T, axis=0, keepdims=True)
    d_prob = contract(values, cotangent, 1, 1)
    d_scores = (prob * (d_prob - delta)).astype(jnp.bfloat16)
    grad_query = (contract(d_scores, keys, 0, 0) * SCALE).astype(jnp.bfloat16)
    grad_keys = contract(d_scores, queries, 1, 0)
    grad_values = contract(prob_low, cotangent, 1, 0)
    return output, grad_query, grad_keys, grad_values


def row_kernel(
    band, place, mask, q, k, v, d, inner_kv, outer_k, outer_v, far_v,
    out, dq, dk, dv, inner_grads, outer_dk, outer_dv, keys, values, acc_k, acc_v,
):
    tokens = q.shape[0]
    rim = outer_k.shape[0]
    odd_device = place[1]
    inner = pl.ds(pl.multiple_of((1 - odd_device) * (rim + tokens), GRIDC), rim)
    outer = pl.ds(pl.multiple_of(odd_device * (rim + tokens), GRIDC), rim)
    keys[rim : rim + tokens] = k[...]
    values[rim : rim + tokens] = v[...]
    keys[inner] = inner_kv[0]
    values[inner] = inner_kv[1]
    keys[outer] = outer_k[...]

    @pl.when(place[2] == 0)
    def _():
        values[outer] = outer_v[...]

    @pl.when(place[2] == 1)
    def _():
        values[outer] = far_v[...]

    acc_k[...] = jnp.zeros_like(acc_k)
    acc_v[...] = jnp.zeros_like(acc_v)
    blocks = 2 * band + 2
    odd = lax.broadcasted_iota(jnp.int32, (1, 2 * GRIDC), 1) >= GRIDC
    total = mask.shape[0]

    def block_bias(row, block):
        key_row = row - band + block
        inside = (key_row >= 0) & (key_row < total)
        sides = []
        for side in range(2):
            offset = block - side
            seen = inside & (mask[row + side, offset] == 1) if 0 <= offset <= 2 * band else False
            sides.append(jnp.where(seen, 0.0, MASKED).astype(jnp.float32))
        return jnp.where(odd, sides[1], sides[0])

    for pair in range(tokens // (2 * GRIDC)):
        here = pl.ds(pair * 2 * GRIDC, 2 * GRIDC)
        window = pl.ds(pair * 2 * GRIDC, blocks * GRIDC)

        def add_bias(scores):
            return jnp.concatenate(
                [
                    scores[b * GRIDC : (b + 1) * GRIDC] + block_bias(place[0] + 2 * pair, b)
                    for b in range(blocks)
                ],
                axis=0,
            )

        output, grad_query, grad_keys, grad_values = attend(
            q[here], d[here], keys[window], values[window], add_bias
        )
        out[here] = output
        dq[here] = grad_query
        acc_k[window] += grad_keys
        acc_v[window] += grad_values
    sides = ((acc_k, dk, outer_dk, SCALE), (acc_v, dv, outer_dv, 1.0))
    for at, (acc, own, across, factor) in enumerate(sides):
        own[...] = acc[rim : rim + tokens] * factor
        inner_grads[at] = (acc[inner] * factor).astype(across.dtype)
        across[...] = (acc[outer] * factor).astype(across.dtype)


def row_attention(place, mask, q, k, v, d, halos, band):
    tokens, feat = q.shape
    heads = feat // HEAD_DIM
    rim = band * GRIDC
    tall = pl.BlockSpec((tokens, HEAD_DIM), lambda h: (0, h))
    edge = pl.BlockSpec((rim, HEAD_DIM), lambda h: (0, h))
    both = pl.BlockSpec((2, rim, HEAD_DIM), lambda h: (0, 0, h))
    scalars = pl.BlockSpec(memory_space=pltpu.SMEM)
    padded = tokens + 2 * rim
    pairs = tokens * (2 * band + 2) * GRIDC * heads
    return pl.pallas_call(
        functools.partial(row_kernel, band),
        grid=(heads,),
        in_specs=[scalars, scalars, tall, tall, tall, tall, both, edge, edge, edge],
        out_specs=[tall] * 4 + [both, edge, edge],
        out_shape=[
            jax.ShapeDtypeStruct(q.shape, jnp.bfloat16),
            jax.ShapeDtypeStruct(q.shape, jnp.bfloat16),
            jax.ShapeDtypeStruct(q.shape, jnp.float32),
            jax.ShapeDtypeStruct(q.shape, jnp.float32),
            jax.ShapeDtypeStruct((2, rim, feat), jnp.bfloat16),
            jax.ShapeDtypeStruct((rim, feat), jnp.bfloat16),
            jax.ShapeDtypeStruct((rim, feat), jnp.bfloat16),
        ],
        scratch_shapes=[
            pltpu.VMEM((padded, HEAD_DIM), jnp.bfloat16),
            pltpu.VMEM((padded, HEAD_DIM), jnp.bfloat16),
            pltpu.VMEM((padded, HEAD_DIM), jnp.float32),
            pltpu.VMEM((padded, HEAD_DIM), jnp.float32),
        ],
        compiler_params=pltpu.CompilerParams(vmem_limit_bytes=VMEM),
        cost_estimate=pl.CostEstimate(
            flops=240 * pairs * HEAD_DIM, bytes_accessed=30 * tokens * feat, transcendentals=pairs
        ),
        name="row_heads",
    )(place, mask, q, k, v, d, *halos)


def col_kernel(n_parts, me, mask, x, earlier, *refs):
    outs, result, bias = refs[:n_parts], refs[n_parts], refs[-1]
    del earlier

    @pl.when((pl.program_id(0) == 0) & (pl.program_id(1) == 0))
    def _():
        size, total = bias.shape[0], mask.shape[0]
        row_of = lax.broadcasted_iota(jnp.int32, (size, total), 0) // GROUP
        spread = (row_of == lax.broadcasted_iota(jnp.int32, (size, total), 1)).astype(jnp.bfloat16)
        seen = (mask[...] == 1).astype(jnp.bfloat16)
        by_key = contract(spread, seen, 1, 1).astype(jnp.bfloat16)
        allowed = contract(by_key, spread, 1, 1)
        key_col = lax.broadcasted_iota(jnp.int32, (size, size), 0) % GROUP
        query_col = lax.broadcasted_iota(jnp.int32, (size, size), 1) % GROUP
        bias[...] = jnp.where((key_col == query_col) & (allowed > 0.5), 0.0, MASKED)

    shape = (x.shape[0], *x.shape[2:])
    tokens = shape[0] * shape[1] * shape[2]
    q, k, v, d = (x[:, a].reshape(tokens, HEAD_DIM) for a in range(4))
    chunk = min(tokens, 256)
    grad_keys, grad_values = 0.0, 0.0
    outputs, grads = [], []
    for start in range(0, tokens, chunk):
        here = slice(start, start + chunk)
        output, grad_query, more_keys, more_values = attend(
            q[here], d[here], k, v, lambda s: s + bias[:, here]
        )
        grad_keys += more_keys
        grad_values += more_values
        outputs.append(output)
        grads.append(grad_query)
    result[:, 0] = jnp.concatenate(outputs, 0).reshape(shape)
    result[:, 1] = jnp.concatenate(grads, 0).reshape(shape)
    result[:, 2] = (grad_keys * SCALE).astype(jnp.bfloat16).reshape(shape)
    result[:, 3] = grad_values.astype(jnp.bfloat16).reshape(shape)
    for partner, out in enumerate(outs):
        out[...] = result[me[0] ^ partner]


def col_attention(me, mask, x, earlier, start, heads, in_parts):
    n, k, rows, cols, _ = x.shape
    n_parts = n if in_parts else 0
    tokens = n * rows * GROUP
    block = (k, rows, GROUP, HEAD_DIM)
    pairs = tokens * tokens * heads * (cols // GROUP)
    part = (k, rows, cols, heads * HEAD_DIM)
    if in_parts:
        out_specs = [pl.BlockSpec(block, lambda h, g: (0, 0, g, h))] * n
        out_shape = [jax.ShapeDtypeStruct(part, jnp.bfloat16)] * n
        held = [pltpu.VMEM((n, *block), jnp.bfloat16)]
    else:
        out_specs = pl.BlockSpec((n, *block), lambda h, g: (0, 0, 0, g, h))
        out_shape = jax.ShapeDtypeStruct((n, *part), jnp.bfloat16)
        held = []
    return pl.pallas_call(
        functools.partial(col_kernel, n_parts),
        grid=(heads, cols // GROUP),
        in_specs=[
            pl.BlockSpec(memory_space=pltpu.SMEM),
            pl.BlockSpec(mask.shape, lambda h, g: (0, 0)),
            pl.BlockSpec((n, *block), lambda h, g: (0, 0, 0, g, h + start)),
            pl.BlockSpec(memory_space=pl.ANY),
        ],
        out_specs=out_specs,
        out_shape=out_shape,
        scratch_shapes=held + [pltpu.VMEM((tokens, tokens), jnp.float32)],
        compiler_params=pltpu.CompilerParams(vmem_limit_bytes=VMEM),
        cost_estimate=pl.CostEstimate(
            flops=240 * pairs * HEAD_DIM, bytes_accessed=4 * x.size, transcendentals=pairs
        ),
        name="col_heads",
    )(me, mask, x, earlier)


def pack_kernel(n, *refs):
    *parts, out, held, arrived, left = refs
    cols = GRIDC // n
    loads = [
        pltpu.make_async_copy(part, held.at[a], arrived.at[a]) for a, part in enumerate(parts)
    ]
    stores = [
        [
            pltpu.make_async_copy(
                held.at[a, :, j * cols : (j + 1) * cols, :], out.at[j, a], left.at[a, j]
            )
            for j in range(n)
        ]
        for a in range(len(parts))
    ]
    for load in loads:
        load.start()
    for load, several in zip(loads, stores):
        load.wait()
        for store in several:
            store.start()
    for several in stores:
        for store in several:
            store.wait()


def packed(arrays, n):
    tokens, feat = arrays[0].shape
    rows, cols, k = tokens // GRIDC, GRIDC // n, len(arrays)
    return pl.pallas_call(
        functools.partial(pack_kernel, n),
        in_specs=[pl.BlockSpec(memory_space=pl.ANY)] * k,
        out_specs=pl.BlockSpec(memory_space=pl.ANY),
        out_shape=jax.ShapeDtypeStruct((n, k, rows, cols, feat), jnp.bfloat16),
        scratch_shapes=[
            pltpu.VMEM((k, rows, GRIDC, feat), jnp.bfloat16),
            pltpu.SemaphoreType.DMA((k,)),
            pltpu.SemaphoreType.DMA((k, n)),
        ],
        compiler_params=pltpu.CompilerParams(vmem_limit_bytes=VMEM),
        cost_estimate=pl.CostEstimate(
            flops=0, bytes_accessed=4 * k * tokens * feat, transcendentals=0
        ),
        name="pack",
    )(*(a.reshape(rows, GRIDC, feat) for a in arrays))


def unpack_kernel(in_parts, n, start, me, *refs):
    held, arrived, left = refs[-3:]
    k, _, _, width = held.shape
    outs = refs[-3 - k : -3]
    cols = GRIDC // n
    loads, stores = [], []
    for a, out in enumerate(outs):
        for i in range(n):
            if in_parts:
                part, source = refs[i], me[0] ^ i
            else:
                part, source = refs[0].at[i], i
            here = pl.ds(pl.multiple_of(source * cols, cols), cols)
            loads.append(
                pltpu.make_async_copy(part.at[a], held.at[a, :, here, :], arrived.at[a, i])
            )
        stores.append(
            pltpu.make_async_copy(held.at[a], out.at[:, :, start : start + width], left.at[a])
        )
    for load in loads:
        load.start()
    for a, store in enumerate(stores):
        for load in loads[a * n : (a + 1) * n]:
            load.wait()
        store.start()
    for store in stores:
        store.wait()


def unpacked(me, parts, start, feat, kept):
    in_parts = isinstance(parts, list)
    parts = parts if in_parts else [parts]
    k, rows, cols, width = parts[0].shape[-4:]
    n = GRIDC // cols
    kept = [a.reshape(rows, GRIDC, feat) for a in kept]
    outs = pl.pallas_call(
        functools.partial(unpack_kernel, in_parts, n, start),
        in_specs=[pl.BlockSpec(memory_space=pltpu.SMEM)]
        + [pl.BlockSpec(memory_space=pl.ANY)] * (len(parts) + len(kept)),
        out_specs=[pl.BlockSpec(memory_space=pl.ANY)] * k,
        out_shape=[jax.ShapeDtypeStruct((rows, GRIDC, feat), jnp.bfloat16)] * k,
        scratch_shapes=[
            pltpu.VMEM((k, rows, GRIDC, width), jnp.bfloat16),
            pltpu.SemaphoreType.DMA((k, n)),
            pltpu.SemaphoreType.DMA((k,)),
        ],
        input_output_aliases={1 + len(parts) + a: a for a in range(len(kept))},
        compiler_params=pltpu.CompilerParams(vmem_limit_bytes=VMEM),
        cost_estimate=pl.CostEstimate(
            flops=0, bytes_accessed=4 * k * rows * GRIDC * width, transcendentals=0
        ),
        name="unpack",
    )(me, *parts, *kept)
    return [o.reshape(rows * GRIDC, feat) for o in outs]


def swapped(inner, outer_k, outer_v):
    n = lax.axis_size("ctx")
    across = [(i, i + 1) for i in range(1, n - 1, 2)]
    far = [(i, j) for i, j in across if j % CHIPS_APART == 0 and j + CHIPS_APART <= n]
    near = [pair for pair in across if pair not in far]
    back = lambda pairs: [(j, i) for i, j in pairs]
    step = CHIPS_APART
    first = [(i, i + step) for i, _ in far] + [(j, j - step) for _, j in far]
    second = [(i + step, j) for i, j in far] + [(j - step, i) for i, j in far]
    outer_v = lax.ppermute(outer_v, "ctx", near + back(near) + first)
    outer_k = lax.ppermute(outer_k, "ctx", across + back(across))
    inner = lax.ppermute(inner, "ctx", [(i, i ^ 1) for i in range(n)])
    return inner, outer_k, outer_v, lambda passed: lax.ppermute(passed, "ctx", second)


def exchanged(x):
    return lax.all_to_all(x, "ctx", 0, 0, tiled=True)


def body(
    row_query, row_key, row_value, row_cotangent, row_mask,
    col_query, col_key, col_value, col_cotangent, col_mask,
):
    n = lax.axis_size("ctx")
    tokens = row_query.shape[0]
    rows = tokens // GRIDC
    band = (row_mask.shape[1] - 1) // 2
    rim = band * GRIDC

    feat = row_key.shape[1]
    me = lax.axis_index("ctx")
    odd = me % 2
    side = me % CHIPS_APART
    inner_at, outer_at = (1 - odd) * (tokens - rim), odd * (tokens - rim)
    rim_of = lambda x, at: lax.dynamic_slice_in_dim(x, at, rim, 0)
    inner = jnp.stack([rim_of(row_key, inner_at), rim_of(row_value, inner_at)])
    outer_k, outer_v = rim_of(row_key, outer_at), rim_of(row_value, outer_at)
    cols = [col_query, col_key, col_value, col_cotangent]
    inner, outer_k, outer_v, cols = lax.optimization_barrier((inner, outer_k, outer_v, cols))
    inner, outer_k, outer_v, second_hop = swapped(inner, outer_k, outer_v)
    sent, outer_v = lax.optimization_barrier((packed(cols, n), outer_v))
    halos = [inner, outer_k, outer_v, second_hop(outer_v)]
    moved = exchanged(sent)

    is_far = (side == 0) | (side == CHIPS_APART - 1)
    place = jnp.stack([me * rows, odd, is_far.astype(odd.dtype)])
    row_output, row_dquery, own_k, own_v, *sides = row_attention(
        place, row_mask, row_query, row_key, row_value, row_cotangent, halos, band
    )
    inner, outer_k, outer_v, second_hop = swapped(*sides)

    heads = col_query.shape[1] // HEAD_DIM
    half = heads // 2
    where = me.reshape(1)
    partners = [[(i, i ^ k) for i in range(n)] for k in range(n)]
    send = lambda parts: [parts[0]] + [
        lax.ppermute(part, "ctx", pairs) for part, pairs in zip(parts[1:], partners[1:])
    ]
    first = col_attention(where, col_mask, moved, row_output, 0, half, False)
    first, inner, outer_k = lax.optimization_barrier((first, inner, outer_k))
    second = col_attention(where, col_mask, moved, first, half, heads - half, True)
    second, outer_v = lax.optimization_barrier((second, outer_v))
    first, second = exchanged(first), send(second)
    col_feat = col_query.shape[1]
    col_results = unpacked(where, first, 0, col_feat, [])
    col_results = unpacked(where, second, half * HEAD_DIM, col_feat, col_results)

    outer_v = jnp.where(is_far, second_hop(outer_v), outer_v)
    row_grads = []
    for own, near, across in ((own_k, inner[0], outer_k), (own_v, inner[1], outer_v)):
        lo = jnp.where(odd == 1, near, across).astype(own.dtype)
        hi = jnp.where(odd == 1, across, near).astype(own.dtype)
        gap = jnp.zeros((tokens - rim, feat), own.dtype)
        added = jnp.concatenate([lo, gap]) + jnp.concatenate([gap, hi])
        row_grads.append((own + added).astype(jnp.bfloat16))
    return (
        row_output, row_dquery, *row_grads,
        *col_results,
    )


def solution(mesh):
    tokens, whole = P("ctx", "head"), P()
    return jax.shard_map(
        body,
        mesh=mesh,
        in_specs=(tokens,) * 4 + (whole,) + (tokens,) * 4 + (whole,),
        out_specs=(tokens,) * 8,
        check_vma=False,
    )
```

```python
import functools

import jax
import jax.numpy as jnp
import numpy as np
from jax import lax
from jax.experimental import pallas as pl
from jax.experimental.pallas import tpu as pltpu
from jax.sharding import PartitionSpec as P

HEAD_DIM = 128
GRIDC = 128
GROUP = 8
MASKED = -1e30
SCALE = HEAD_DIM**-0.5
EXP2_SCALE = SCALE * float(np.log2(np.e))
VMEM = 60 << 20
CHIPS_APART = 4


def contract(a, b, dim_a, dim_b):
    return lax.dot_general(
        a, b, (((dim_a,), (dim_b,)), ((), ())), preferred_element_type=jnp.float32
    )


def attend(queries, cotangent, keys, values, add_bias):
    n_keys, n_queries = keys.shape[0], queries.shape[0]
    scores = add_bias(contract(keys, queries, 1, 1))
    top = jnp.max(scores, axis=0, keepdims=True)
    terms = jnp.exp2((scores - top) * EXP2_SCALE)
    prob = terms * (1.0 / jnp.sum(terms, axis=0, keepdims=True))
    prob_low = prob.astype(jnp.bfloat16)
    output = contract(prob_low, values, 0, 0).astype(jnp.bfloat16)
    product = cotangent.astype(jnp.float32) * output.astype(jnp.float32)
    delta = jnp.sum(product.T, axis=0, keepdims=True)
    d_prob = contract(values, cotangent, 1, 1)
    d_scores = (prob * (d_prob - delta)).astype(jnp.bfloat16)
    grad_query = (contract(d_scores, keys, 0, 0) * SCALE).astype(jnp.bfloat16)
    grad_keys = contract(d_scores, queries, 1, 0)
    grad_values = contract(prob_low, cotangent, 1, 0)
    return output, grad_query, grad_keys, grad_values


def row_kernel(
    band, place, mask, q, k, v, d, inner_kv, outer_k, outer_v, far_v,
    out, dq, dk, dv, inner_grads, outer_dk, outer_dv, keys, values, acc_k, acc_v,
):
    tokens = q.shape[0]
    rim = outer_k.shape[0]
    odd_device = place[1]
    inner = pl.ds(pl.multiple_of((1 - odd_device) * (rim + tokens), GRIDC), rim)
    outer = pl.ds(pl.multiple_of(odd_device * (rim + tokens), GRIDC), rim)
    keys[rim : rim + tokens] = k[...]
    values[rim : rim + tokens] = v[...]
    keys[inner] = inner_kv[0]
    values[inner] = inner_kv[1]
    keys[outer] = outer_k[...]

    @pl.when(place[2] == 0)
    def _():
        values[outer] = outer_v[...]

    @pl.when(place[2] == 1)
    def _():
        values[outer] = far_v[...]

    acc_k[...] = jnp.zeros_like(acc_k)
    acc_v[...] = jnp.zeros_like(acc_v)
    blocks = 2 * band + 2
    odd = lax.broadcasted_iota(jnp.int32, (1, 2 * GRIDC), 1) >= GRIDC
    total = mask.shape[0]

    def block_bias(row, block):
        key_row = row - band + block
        inside = (key_row >= 0) & (key_row < total)
        sides = []
        for side in range(2):
            offset = block - side
            seen = inside & (mask[row + side, offset] == 1) if 0 <= offset <= 2 * band else False
            sides.append(jnp.where(seen, 0.0, MASKED).astype(jnp.float32))
        return jnp.where(odd, sides[1], sides[0])

    for pair in range(tokens // (2 * GRIDC)):
        here = pl.ds(pair * 2 * GRIDC, 2 * GRIDC)
        window = pl.ds(pair * 2 * GRIDC, blocks * GRIDC)

        def add_bias(scores):
            return jnp.concatenate(
                [
                    scores[b * GRIDC : (b + 1) * GRIDC] + block_bias(place[0] + 2 * pair, b)
                    for b in range(blocks)
                ],
                axis=0,
            )

        output, grad_query, grad_keys, grad_values = attend(
            q[here], d[here], keys[window], values[window], add_bias
        )
        out[here] = output
        dq[here] = grad_query
        acc_k[window] += grad_keys
        acc_v[window] += grad_values
    sides = ((acc_k, dk, outer_dk, SCALE), (acc_v, dv, outer_dv, 1.0))
    for at, (acc, own, across, factor) in enumerate(sides):
        own[...] = acc[rim : rim + tokens] * factor
        inner_grads[at] = (acc[inner] * factor).astype(across.dtype)
        across[...] = (acc[outer] * factor).astype(across.dtype)


def row_attention(place, mask, q, k, v, d, halos, band):
    tokens, feat = q.shape
    heads = feat // HEAD_DIM
    rim = band * GRIDC
    tall = pl.BlockSpec((tokens, HEAD_DIM), lambda h: (0, h))
    edge = pl.BlockSpec((rim, HEAD_DIM), lambda h: (0, h))
    both = pl.BlockSpec((2, rim, HEAD_DIM), lambda h: (0, 0, h))
    scalars = pl.BlockSpec(memory_space=pltpu.SMEM)
    padded = tokens + 2 * rim
    pairs = tokens * (2 * band + 2) * GRIDC * heads
    return pl.pallas_call(
        functools.partial(row_kernel, band),
        grid=(heads,),
        in_specs=[scalars, scalars, tall, tall, tall, tall, both, edge, edge, edge],
        out_specs=[tall] * 4 + [both, edge, edge],
        out_shape=[
            jax.ShapeDtypeStruct(q.shape, jnp.bfloat16),
            jax.ShapeDtypeStruct(q.shape, jnp.bfloat16),
            jax.ShapeDtypeStruct(q.shape, jnp.float32),
            jax.ShapeDtypeStruct(q.shape, jnp.float32),
            jax.ShapeDtypeStruct((2, rim, feat), jnp.bfloat16),
            jax.ShapeDtypeStruct((rim, feat), jnp.bfloat16),
            jax.ShapeDtypeStruct((rim, feat), jnp.bfloat16),
        ],
        scratch_shapes=[
            pltpu.VMEM((padded, HEAD_DIM), jnp.bfloat16),
            pltpu.VMEM((padded, HEAD_DIM), jnp.bfloat16),
            pltpu.VMEM((padded, HEAD_DIM), jnp.float32),
            pltpu.VMEM((padded, HEAD_DIM), jnp.float32),
        ],
        compiler_params=pltpu.CompilerParams(vmem_limit_bytes=VMEM),
        cost_estimate=pl.CostEstimate(
            flops=240 * pairs * HEAD_DIM, bytes_accessed=30 * tokens * feat, transcendentals=pairs
        ),
        name="row_heads",
    )(place, mask, q, k, v, d, *halos)


def col_kernel(n_parts, me, mask, x, earlier, *refs):
    outs, result, bias = refs[:n_parts], refs[n_parts], refs[-1]
    del earlier

    @pl.when((pl.program_id(0) == 0) & (pl.program_id(1) == 0))
    def _():
        size, total = bias.shape[0], mask.shape[0]
        row_of = lax.broadcasted_iota(jnp.int32, (size, total), 0) // GROUP
        spread = (row_of == lax.broadcasted_iota(jnp.int32, (size, total), 1)).astype(jnp.bfloat16)
        seen = (mask[...] == 1).astype(jnp.bfloat16)
        by_key = contract(spread, seen, 1, 1).astype(jnp.bfloat16)
        allowed = contract(by_key, spread, 1, 1)
        key_col = lax.broadcasted_iota(jnp.int32, (size, size), 0) % GROUP
        query_col = lax.broadcasted_iota(jnp.int32, (size, size), 1) % GROUP
        bias[...] = jnp.where((key_col == query_col) & (allowed > 0.5), 0.0, MASKED)

    shape = (x.shape[0], *x.shape[2:])
    tokens = shape[0] * shape[1] * shape[2]
    q, k, v, d = (x[:, a].reshape(tokens, HEAD_DIM) for a in range(4))
    chunk = min(tokens, 256)
    grad_keys, grad_values = 0.0, 0.0
    outputs, grads = [], []
    for start in range(0, tokens, chunk):
        here = slice(start, start + chunk)
        output, grad_query, more_keys, more_values = attend(
            q[here], d[here], k, v, lambda s: s + bias[:, here]
        )
        grad_keys += more_keys
        grad_values += more_values
        outputs.append(output)
        grads.append(grad_query)
    result[:, 0] = jnp.concatenate(outputs, 0).reshape(shape)
    result[:, 1] = jnp.concatenate(grads, 0).reshape(shape)
    result[:, 2] = (grad_keys * SCALE).astype(jnp.bfloat16).reshape(shape)
    result[:, 3] = grad_values.astype(jnp.bfloat16).reshape(shape)
    for partner, out in enumerate(outs):
        out[...] = result[me[0] ^ partner]


def col_attention(me, mask, x, earlier, start, heads, in_parts):
    n, k, rows, cols, _ = x.shape
    n_parts = n if in_parts else 0
    tokens = n * rows * GROUP
    block = (k, rows, GROUP, HEAD_DIM)
    pairs = tokens * tokens * heads * (cols // GROUP)
    part = (k, rows, cols, heads * HEAD_DIM)
    if in_parts:
        out_specs = [pl.BlockSpec(block, lambda h, g: (0, 0, g, h))] * n
        out_shape = [jax.ShapeDtypeStruct(part, jnp.bfloat16)] * n
        held = [pltpu.VMEM((n, *block), jnp.bfloat16)]
    else:
        out_specs = pl.BlockSpec((n, *block), lambda h, g: (0, 0, 0, g, h))
        out_shape = jax.ShapeDtypeStruct((n, *part), jnp.bfloat16)
        held = []
    return pl.pallas_call(
        functools.partial(col_kernel, n_parts),
        grid=(heads, cols // GROUP),
        in_specs=[
            pl.BlockSpec(memory_space=pltpu.SMEM),
            pl.BlockSpec(mask.shape, lambda h, g: (0, 0)),
            pl.BlockSpec((n, *block), lambda h, g: (0, 0, 0, g, h + start)),
            pl.BlockSpec(memory_space=pl.ANY),
        ],
        out_specs=out_specs,
        out_shape=out_shape,
        scratch_shapes=held + [pltpu.VMEM((tokens, tokens), jnp.float32)],
        compiler_params=pltpu.CompilerParams(vmem_limit_bytes=VMEM),
        cost_estimate=pl.CostEstimate(
            flops=240 * pairs * HEAD_DIM, bytes_accessed=4 * x.size, transcendentals=pairs
        ),
        name="col_heads",
    )(me, mask, x, earlier)


def pack_kernel(n, *refs):
    *parts, out, held, arrived, left = refs
    cols = GRIDC // n
    loads = [
        pltpu.make_async_copy(part, held.at[a], arrived.at[a]) for a, part in enumerate(parts)
    ]
    stores = [
        [
            pltpu.make_async_copy(
                held.at[a, :, j * cols : (j + 1) * cols, :], out.at[j, a], left.at[a, j]
            )
            for j in range(n)
        ]
        for a in range(len(parts))
    ]
    for load in loads:
        load.start()
    for load, several in zip(loads, stores):
        load.wait()
        for store in several:
            store.start()
    for several in stores:
        for store in several:
            store.wait()


def packed(arrays, n):
    tokens, feat = arrays[0].shape
    rows, cols, k = tokens // GRIDC, GRIDC // n, len(arrays)
    return pl.pallas_call(
        functools.partial(pack_kernel, n),
        in_specs=[pl.BlockSpec(memory_space=pl.ANY)] * k,
        out_specs=pl.BlockSpec(memory_space=pl.ANY),
        out_shape=jax.ShapeDtypeStruct((n, k, rows, cols, feat), jnp.bfloat16),
        scratch_shapes=[
            pltpu.VMEM((k, rows, GRIDC, feat), jnp.bfloat16),
            pltpu.SemaphoreType.DMA((k,)),
            pltpu.SemaphoreType.DMA((k, n)),
        ],
        compiler_params=pltpu.CompilerParams(vmem_limit_bytes=VMEM),
        cost_estimate=pl.CostEstimate(
            flops=0, bytes_accessed=4 * k * tokens * feat, transcendentals=0
        ),
        name="pack",
    )(*(a.reshape(rows, GRIDC, feat) for a in arrays))


def unpack_kernel(partners, start, me, *refs):
    held, arrived, left = refs[-3:]
    count, k, _, cols, width = held.shape
    outs = refs[-3 - k : -3]
    loads, stores = [], []
    for i in range(count):
        part, source = (refs[0].at[i], i) if partners is None else (refs[i], me[0] ^ partners[i])
        here = pl.ds(pl.multiple_of(source * cols, cols), cols)
        loads.append(pltpu.make_async_copy(part, held.at[i], arrived.at[i]))
        stores += [
            pltpu.make_async_copy(
                held.at[i, a], out.at[:, here, start : start + width], left.at[i, a]
            )
            for a, out in enumerate(outs)
        ]
    for load in loads:
        load.start()
    for i, load in enumerate(loads):
        load.wait()
        for store in stores[i * k : (i + 1) * k]:
            store.start()
    for store in stores:
        store.wait()


def unpacked(me, parts, partners, start, feat, kept):
    parts = [parts] if partners is None else parts
    k, rows, cols, width = parts[0].shape[-4:]
    count = GRIDC // cols if partners is None else len(parts)
    kept = [a.reshape(rows, GRIDC, feat) for a in kept]
    outs = pl.pallas_call(
        functools.partial(unpack_kernel, partners, start),
        in_specs=[pl.BlockSpec(memory_space=pltpu.SMEM)]
        + [pl.BlockSpec(memory_space=pl.ANY)] * (len(parts) + len(kept)),
        out_specs=[pl.BlockSpec(memory_space=pl.ANY)] * k,
        out_shape=[jax.ShapeDtypeStruct((rows, GRIDC, feat), jnp.bfloat16)] * k,
        scratch_shapes=[
            pltpu.VMEM((count, k, rows, cols, width), jnp.bfloat16),
            pltpu.SemaphoreType.DMA((count,)),
            pltpu.SemaphoreType.DMA((count, k)),
        ],
        input_output_aliases={1 + len(parts) + a: a for a in range(len(kept))},
        compiler_params=pltpu.CompilerParams(vmem_limit_bytes=VMEM),
        cost_estimate=pl.CostEstimate(
            flops=0, bytes_accessed=4 * k * rows * count * cols * width, transcendentals=0
        ),
        name="unpack",
    )(me, *parts, *kept)
    return [o.reshape(rows * GRIDC, feat) for o in outs]


def swapped(inner, outer_k, outer_v):
    n = lax.axis_size("ctx")
    across = [(i, i + 1) for i in range(1, n - 1, 2)]
    far = [(i, j) for i, j in across if j % CHIPS_APART == 0 and j + CHIPS_APART <= n]
    near = [pair for pair in across if pair not in far]
    back = lambda pairs: [(j, i) for i, j in pairs]
    step = CHIPS_APART
    first = [(i, i + step) for i, _ in far] + [(j, j - step) for _, j in far]
    second = [(i + step, j) for i, j in far] + [(j - step, i) for i, j in far]
    outer_v = lax.ppermute(outer_v, "ctx", near + back(near) + first)
    outer_k = lax.ppermute(outer_k, "ctx", across + back(across))
    inner = lax.ppermute(inner, "ctx", [(i, i ^ 1) for i in range(n)])
    return inner, outer_k, outer_v, lambda passed: lax.ppermute(passed, "ctx", second)


def exchanged(x):
    return lax.all_to_all(x, "ctx", 0, 0, tiled=True)


def body(
    row_query, row_key, row_value, row_cotangent, row_mask,
    col_query, col_key, col_value, col_cotangent, col_mask,
):
    n = lax.axis_size("ctx")
    tokens = row_query.shape[0]
    rows = tokens // GRIDC
    band = (row_mask.shape[1] - 1) // 2
    rim = band * GRIDC

    feat = row_key.shape[1]
    me = lax.axis_index("ctx")
    odd = me % 2
    side = me % CHIPS_APART
    inner_at, outer_at = (1 - odd) * (tokens - rim), odd * (tokens - rim)
    rim_of = lambda x, at: lax.dynamic_slice_in_dim(x, at, rim, 0)
    cols = [col_query, col_key, col_value, col_cotangent]
    outer_v = rim_of(row_value, outer_at)
    outer_v, key, value, cols = lax.optimization_barrier((outer_v, row_key, row_value, cols))
    outer_k = rim_of(key, outer_at)
    inner = jnp.stack([rim_of(key, inner_at), rim_of(value, inner_at)])
    inner, outer_k, outer_v, second_hop = swapped(inner, outer_k, outer_v)
    sent, outer_v = lax.optimization_barrier((packed(cols, n), outer_v))
    halos = [inner, outer_k, outer_v, second_hop(outer_v)]
    moved = exchanged(sent)

    is_far = (side == 0) | (side == CHIPS_APART - 1)
    place = jnp.stack([me * rows, odd, is_far.astype(odd.dtype)])
    row_output, row_dquery, own_k, own_v, *sides = row_attention(
        place, row_mask, row_query, row_key, row_value, row_cotangent, halos, band
    )
    inner, outer_k, outer_v, second_hop = swapped(*sides)

    heads = col_query.shape[1] // HEAD_DIM
    half = heads // 3
    where = me.reshape(1)
    partners = [[(i, i ^ k) for i in range(n)] for k in range(n)]
    first = col_attention(where, col_mask, moved, row_output, 0, half, False)
    first, inner, outer_k = lax.optimization_barrier((first, inner, outer_k))
    second = col_attention(where, col_mask, moved, first, half, heads - half, True)
    second, outer_v = lax.optimization_barrier((second, outer_v))
    first = exchanged(first)
    arrived = [second[0]] + [
        lax.ppermute(second[k], "ctx", partners[k]) for k in range(1, n - 2)
    ]
    *last, arrived[2] = lax.optimization_barrier((second[n - 2], second[n - 1], arrived[2]))
    arrived += [lax.ppermute(part, "ctx", pairs) for part, pairs in zip(last, partners[n - 2 :])]
    col_feat = col_query.shape[1]
    col_results = unpacked(where, first, None, 0, col_feat, [])
    for some in (list(range(n - 2)), [n - 2, n - 1]):
        col_results = unpacked(
            where, [arrived[k] for k in some], some, half * HEAD_DIM, col_feat, col_results
        )

    outer_v = jnp.where(is_far, second_hop(outer_v), outer_v)
    row_grads = []
    for own, near, across in ((own_k, inner[0], outer_k), (own_v, inner[1], outer_v)):
        lo = jnp.where(odd == 1, near, across).astype(own.dtype)
        hi = jnp.where(odd == 1, across, near).astype(own.dtype)
        gap = jnp.zeros((tokens - rim, feat), own.dtype)
        added = jnp.concatenate([lo, gap]) + jnp.concatenate([gap, hi])
        row_grads.append((own + added).astype(jnp.bfloat16))
    return (
        row_output, row_dquery, *row_grads,
        *col_results,
    )


def solution(mesh):
    tokens, whole = P("ctx", "head"), P()
    return jax.shard_map(
        body,
        mesh=mesh,
        in_specs=(tokens,) * 4 + (whole,) + (tokens,) * 4 + (whole,),
        out_specs=(tokens,) * 8,
        check_vma=False,
    )
```

```python
import functools

import jax
import jax.numpy as jnp
import numpy as np
from jax import lax
from jax.experimental import pallas as pl
from jax.experimental.pallas import tpu as pltpu
from jax.sharding import PartitionSpec as P

HEAD_DIM = 128
GRIDC = 128
GROUP = 8
MASKED = -1e30
SCALE = HEAD_DIM**-0.5
EXP2_SCALE = SCALE * float(np.log2(np.e))
VMEM = 60 << 20
CHIPS_APART = 4


def contract(a, b, dim_a, dim_b):
    return lax.dot_general(
        a, b, (((dim_a,), (dim_b,)), ((), ())), preferred_element_type=jnp.float32
    )


def attend(queries, cotangent, keys, values, add_bias):
    n_keys, n_queries = keys.shape[0], queries.shape[0]
    scores = add_bias(contract(keys, queries, 1, 1))
    top = jnp.max(scores, axis=0, keepdims=True)
    terms = jnp.exp2((scores - top) * EXP2_SCALE)
    prob = terms * (1.0 / jnp.sum(terms, axis=0, keepdims=True))
    prob_low = prob.astype(jnp.bfloat16)
    output = contract(prob_low, values, 0, 0).astype(jnp.bfloat16)
    product = cotangent.astype(jnp.float32) * output.astype(jnp.float32)
    delta = jnp.sum(product.T, axis=0, keepdims=True)
    d_prob = contract(values, cotangent, 1, 1)
    d_scores = (prob * (d_prob - delta)).astype(jnp.bfloat16)
    grad_query = (contract(d_scores, keys, 0, 0) * SCALE).astype(jnp.bfloat16)
    grad_keys = contract(d_scores, queries, 1, 0)
    grad_values = contract(prob_low, cotangent, 1, 0)
    return output, grad_query, grad_keys, grad_values


def row_kernel(
    band, place, mask, q, k, v, d, inner_kv, outer_k, outer_v, far_v,
    out, dq, dk, dv, inner_grads, outer_dk, outer_dv, keys, values, acc_k, acc_v,
):
    tokens = q.shape[0]
    rim = outer_k.shape[0]
    odd_device = place[1]
    inner = pl.ds(pl.multiple_of((1 - odd_device) * (rim + tokens), GRIDC), rim)
    outer = pl.ds(pl.multiple_of(odd_device * (rim + tokens), GRIDC), rim)
    keys[rim : rim + tokens] = k[...]
    values[rim : rim + tokens] = v[...]
    keys[inner] = inner_kv[0]
    values[inner] = inner_kv[1]
    keys[outer] = outer_k[...]

    @pl.when(place[2] == 0)
    def _():
        values[outer] = outer_v[...]

    @pl.when(place[2] == 1)
    def _():
        values[outer] = far_v[...]

    acc_k[...] = jnp.zeros_like(acc_k)
    acc_v[...] = jnp.zeros_like(acc_v)
    blocks = 2 * band + 2
    odd = lax.broadcasted_iota(jnp.int32, (1, 2 * GRIDC), 1) >= GRIDC
    total = mask.shape[0]

    def block_bias(row, block):
        key_row = row - band + block
        inside = (key_row >= 0) & (key_row < total)
        sides = []
        for side in range(2):
            offset = block - side
            seen = inside & (mask[row + side, offset] == 1) if 0 <= offset <= 2 * band else False
            sides.append(jnp.where(seen, 0.0, MASKED).astype(jnp.float32))
        return jnp.where(odd, sides[1], sides[0])

    for pair in range(tokens // (2 * GRIDC)):
        here = pl.ds(pair * 2 * GRIDC, 2 * GRIDC)
        window = pl.ds(pair * 2 * GRIDC, blocks * GRIDC)

        def add_bias(scores):
            return jnp.concatenate(
                [
                    scores[b * GRIDC : (b + 1) * GRIDC] + block_bias(place[0] + 2 * pair, b)
                    for b in range(blocks)
                ],
                axis=0,
            )

        output, grad_query, grad_keys, grad_values = attend(
            q[here], d[here], keys[window], values[window], add_bias
        )
        out[here] = output
        dq[here] = grad_query
        acc_k[window] += grad_keys
        acc_v[window] += grad_values
    sides = ((acc_k, dk, outer_dk, SCALE), (acc_v, dv, outer_dv, 1.0))
    for at, (acc, own, across, factor) in enumerate(sides):
        own[...] = acc[rim : rim + tokens] * factor
        inner_grads[at] = (acc[inner] * factor).astype(across.dtype)
        across[...] = (acc[outer] * factor).astype(across.dtype)


def row_attention(place, mask, q, k, v, d, halos, band):
    tokens, feat = q.shape
    heads = feat // HEAD_DIM
    rim = band * GRIDC
    tall = pl.BlockSpec((tokens, HEAD_DIM), lambda h: (0, h))
    edge = pl.BlockSpec((rim, HEAD_DIM), lambda h: (0, h))
    both = pl.BlockSpec((2, rim, HEAD_DIM), lambda h: (0, 0, h))
    scalars = pl.BlockSpec(memory_space=pltpu.SMEM)
    padded = tokens + 2 * rim
    pairs = tokens * (2 * band + 2) * GRIDC * heads
    return pl.pallas_call(
        functools.partial(row_kernel, band),
        grid=(heads,),
        in_specs=[scalars, scalars, tall, tall, tall, tall, both, edge, edge, edge],
        out_specs=[tall] * 4 + [both, edge, edge],
        out_shape=[
            jax.ShapeDtypeStruct(q.shape, jnp.bfloat16),
            jax.ShapeDtypeStruct(q.shape, jnp.bfloat16),
            jax.ShapeDtypeStruct(q.shape, jnp.float32),
            jax.ShapeDtypeStruct(q.shape, jnp.float32),
            jax.ShapeDtypeStruct((2, rim, feat), jnp.bfloat16),
            jax.ShapeDtypeStruct((rim, feat), jnp.bfloat16),
            jax.ShapeDtypeStruct((rim, feat), jnp.bfloat16),
        ],
        scratch_shapes=[
            pltpu.VMEM((padded, HEAD_DIM), jnp.bfloat16),
            pltpu.VMEM((padded, HEAD_DIM), jnp.bfloat16),
            pltpu.VMEM((padded, HEAD_DIM), jnp.float32),
            pltpu.VMEM((padded, HEAD_DIM), jnp.float32),
        ],
        compiler_params=pltpu.CompilerParams(vmem_limit_bytes=VMEM),
        cost_estimate=pl.CostEstimate(
            flops=240 * pairs * HEAD_DIM, bytes_accessed=30 * tokens * feat, transcendentals=pairs
        ),
        name="row_heads",
    )(place, mask, q, k, v, d, *halos)


def col_kernel(n_parts, me, mask, x, earlier, *refs):
    outs, result, bias = refs[:n_parts], refs[n_parts], refs[-1]
    del earlier

    @pl.when((pl.program_id(0) == 0) & (pl.program_id(1) == 0))
    def _():
        size, total = bias.shape[0], mask.shape[0]
        row_of = lax.broadcasted_iota(jnp.int32, (size, total), 0) // GROUP
        spread = (row_of == lax.broadcasted_iota(jnp.int32, (size, total), 1)).astype(jnp.bfloat16)
        seen = (mask[...] == 1).astype(jnp.bfloat16)
        by_key = contract(spread, seen, 1, 1).astype(jnp.bfloat16)
        allowed = contract(by_key, spread, 1, 1)
        key_col = lax.broadcasted_iota(jnp.int32, (size, size), 0) % GROUP
        query_col = lax.broadcasted_iota(jnp.int32, (size, size), 1) % GROUP
        bias[...] = jnp.where((key_col == query_col) & (allowed > 0.5), 0.0, MASKED)

    shape = (x.shape[0], *x.shape[2:])
    tokens = shape[0] * shape[1] * shape[2]
    q, k, v, d = (x[:, a].reshape(tokens, HEAD_DIM) for a in range(4))
    chunk = min(tokens, 256)
    grad_keys, grad_values = 0.0, 0.0
    outputs, grads = [], []
    for start in range(0, tokens, chunk):
        here = slice(start, start + chunk)
        output, grad_query, more_keys, more_values = attend(
            q[here], d[here], k, v, lambda s: s + bias[:, here]
        )
        grad_keys += more_keys
        grad_values += more_values
        outputs.append(output)
        grads.append(grad_query)
    result[:, 0] = jnp.concatenate(outputs, 0).reshape(shape)
    result[:, 1] = jnp.concatenate(grads, 0).reshape(shape)
    result[:, 2] = (grad_keys * SCALE).astype(jnp.bfloat16).reshape(shape)
    result[:, 3] = grad_values.astype(jnp.bfloat16).reshape(shape)
    for partner, out in enumerate(outs):
        out[...] = result[me[0] ^ partner]


def col_attention(me, mask, x, earlier, start, heads, in_parts):
    n, k, rows, cols, _ = x.shape
    n_parts = n if in_parts else 0
    tokens = n * rows * GROUP
    block = (k, rows, GROUP, HEAD_DIM)
    pairs = tokens * tokens * heads * (cols // GROUP)
    part = (k, rows, cols, heads * HEAD_DIM)
    if in_parts:
        out_specs = [pl.BlockSpec(block, lambda h, g: (0, 0, g, h))] * n
        out_shape = [jax.ShapeDtypeStruct(part, jnp.bfloat16)] * n
        held = [pltpu.VMEM((n, *block), jnp.bfloat16)]
    else:
        out_specs = pl.BlockSpec((n, *block), lambda h, g: (0, 0, 0, g, h))
        out_shape = jax.ShapeDtypeStruct((n, *part), jnp.bfloat16)
        held = []
    return pl.pallas_call(
        functools.partial(col_kernel, n_parts),
        grid=(heads, cols // GROUP),
        in_specs=[
            pl.BlockSpec(memory_space=pltpu.SMEM),
            pl.BlockSpec(mask.shape, lambda h, g: (0, 0)),
            pl.BlockSpec((n, *block), lambda h, g: (0, 0, 0, g, h + start)),
            pl.BlockSpec(memory_space=pl.ANY),
        ],
        out_specs=out_specs,
        out_shape=out_shape,
        scratch_shapes=held + [pltpu.VMEM((tokens, tokens), jnp.float32)],
        compiler_params=pltpu.CompilerParams(vmem_limit_bytes=VMEM),
        cost_estimate=pl.CostEstimate(
            flops=240 * pairs * HEAD_DIM, bytes_accessed=4 * x.size, transcendentals=pairs
        ),
        name="col_heads",
    )(me, mask, x, earlier)


def pack_kernel(n, *refs):
    *parts, out, held, arrived, left = refs
    cols = GRIDC // n
    loads = [
        pltpu.make_async_copy(part, held.at[a], arrived.at[a]) for a, part in enumerate(parts)
    ]
    stores = [
        [
            pltpu.make_async_copy(
                held.at[a, :, j * cols : (j + 1) * cols, :], out.at[j, a], left.at[a, j]
            )
            for j in range(n)
        ]
        for a in range(len(parts))
    ]
    for load in loads:
        load.start()
    for load, several in zip(loads, stores):
        load.wait()
        for store in several:
            store.start()
    for several in stores:
        for store in several:
            store.wait()


def packed(arrays, n):
    tokens, feat = arrays[0].shape
    rows, cols, k = tokens // GRIDC, GRIDC // n, len(arrays)
    return pl.pallas_call(
        functools.partial(pack_kernel, n),
        in_specs=[pl.BlockSpec(memory_space=pl.ANY)] * k,
        out_specs=pl.BlockSpec(memory_space=pl.ANY),
        out_shape=jax.ShapeDtypeStruct((n, k, rows, cols, feat), jnp.bfloat16),
        scratch_shapes=[
            pltpu.VMEM((k, rows, GRIDC, feat), jnp.bfloat16),
            pltpu.SemaphoreType.DMA((k,)),
            pltpu.SemaphoreType.DMA((k, n)),
        ],
        compiler_params=pltpu.CompilerParams(vmem_limit_bytes=VMEM),
        cost_estimate=pl.CostEstimate(
            flops=0, bytes_accessed=4 * k * tokens * feat, transcendentals=0
        ),
        name="pack",
    )(*(a.reshape(rows, GRIDC, feat) for a in arrays))


def unpack_kernel(partners, start, me, *refs):
    held, arrived, left = refs[-3:]
    count, k, _, cols, width = held.shape
    outs = refs[-3 - k : -3]
    loads, stores = [], []
    for i in range(count):
        part, source = (refs[0].at[i], i) if partners is None else (refs[i], me[0] ^ partners[i])
        here = pl.ds(pl.multiple_of(source * cols, cols), cols)
        loads.append(pltpu.make_async_copy(part, held.at[i], arrived.at[i]))
        stores += [
            pltpu.make_async_copy(
                held.at[i, a], out.at[:, here, start : start + width], left.at[i, a]
            )
            for a, out in enumerate(outs)
        ]
    for load in loads:
        load.start()
    for i, load in enumerate(loads):
        load.wait()
        for store in stores[i * k : (i + 1) * k]:
            store.start()
    for store in stores:
        store.wait()


def unpacked(me, parts, partners, start, feat, kept):
    parts = [parts] if partners is None else parts
    k, rows, cols, width = parts[0].shape[-4:]
    count = GRIDC // cols if partners is None else len(parts)
    kept = [a.reshape(rows, GRIDC, feat) for a in kept]
    outs = pl.pallas_call(
        functools.partial(unpack_kernel, partners, start),
        in_specs=[pl.BlockSpec(memory_space=pltpu.SMEM)]
        + [pl.BlockSpec(memory_space=pl.ANY)] * (len(parts) + len(kept)),
        out_specs=[pl.BlockSpec(memory_space=pl.ANY)] * k,
        out_shape=[jax.ShapeDtypeStruct((rows, GRIDC, feat), jnp.bfloat16)] * k,
        scratch_shapes=[
            pltpu.VMEM((count, k, rows, cols, width), jnp.bfloat16),
            pltpu.SemaphoreType.DMA((count,)),
            pltpu.SemaphoreType.DMA((count, k)),
        ],
        input_output_aliases={1 + len(parts) + a: a for a in range(len(kept))},
        compiler_params=pltpu.CompilerParams(vmem_limit_bytes=VMEM),
        cost_estimate=pl.CostEstimate(
            flops=0, bytes_accessed=4 * k * rows * count * cols * width, transcendentals=0
        ),
        name="unpack",
    )(me, *parts, *kept)
    return [o.reshape(rows * GRIDC, feat) for o in outs]


def swapped(inner, outer_k, outer_v):
    n = lax.axis_size("ctx")
    across = [(i, i + 1) for i in range(1, n - 1, 2)]
    far = [(i, j) for i, j in across if j % CHIPS_APART == 0 and j + CHIPS_APART <= n]
    near = [pair for pair in across if pair not in far]
    back = lambda pairs: [(j, i) for i, j in pairs]
    step = CHIPS_APART
    first = [(i, i + step) for i, _ in far] + [(j, j - step) for _, j in far]
    second = [(i + step, j) for i, j in far] + [(j - step, i) for i, j in far]
    hop = lax.ppermute(outer_v, "ctx", first)
    outer_k = lax.ppermute(outer_k, "ctx", across + back(across))
    outer_v = lax.ppermute(outer_v, "ctx", near + back(near))
    inner = lax.ppermute(inner, "ctx", [(i, i ^ 1) for i in range(n)])
    return inner, outer_k, outer_v, hop, lambda passed: lax.ppermute(passed, "ctx", second)


def exchanged(x):
    return lax.all_to_all(x, "ctx", 0, 0, tiled=True)


def body(
    row_query, row_key, row_value, row_cotangent, row_mask,
    col_query, col_key, col_value, col_cotangent, col_mask,
):
    n = lax.axis_size("ctx")
    tokens = row_query.shape[0]
    rows = tokens // GRIDC
    band = (row_mask.shape[1] - 1) // 2
    rim = band * GRIDC

    feat = row_key.shape[1]
    me = lax.axis_index("ctx")
    odd = me % 2
    side = me % CHIPS_APART
    inner_at, outer_at = (1 - odd) * (tokens - rim), odd * (tokens - rim)
    rim_of = lambda x, at: lax.dynamic_slice_in_dim(x, at, rim, 0)
    cols = [col_query, col_key, col_value, col_cotangent]
    inner = jnp.stack([rim_of(row_key, inner_at), rim_of(row_value, inner_at)])
    outer_k, outer_v = rim_of(row_key, outer_at), rim_of(row_value, outer_at)
    inner, outer_k, outer_v, cols = lax.optimization_barrier((inner, outer_k, outer_v, cols))
    inner, outer_k, outer_v, hop, second_hop = swapped(inner, outer_k, outer_v)
    sent, hop = lax.optimization_barrier((packed(cols, n), hop))
    halos = [inner, outer_k, outer_v, second_hop(hop)]
    moved = exchanged(sent)

    is_far = (side == 0) | (side == CHIPS_APART - 1)
    place = jnp.stack([me * rows, odd, is_far.astype(odd.dtype)])
    row_output, row_dquery, own_k, own_v, *sides = row_attention(
        place, row_mask, row_query, row_key, row_value, row_cotangent, halos, band
    )
    inner, outer_k, outer_v, hop, second_hop = swapped(*sides)

    heads = col_query.shape[1] // HEAD_DIM
    half = heads // 3
    where = me.reshape(1)
    partners = [[(i, i ^ k) for i in range(n)] for k in range(n)]
    first = col_attention(where, col_mask, moved, row_output, 0, half, False)
    first, inner, hop = lax.optimization_barrier((first, inner, hop))
    second = col_attention(where, col_mask, moved, first, half, heads - half, True)
    second, outer_k, outer_v = lax.optimization_barrier((second, outer_k, outer_v))
    first = exchanged(first)
    arrived = [second[0]] + [
        lax.ppermute(second[k], "ctx", partners[k]) for k in range(1, n - 2)
    ]
    *last, arrived[2] = lax.optimization_barrier((second[n - 2], second[n - 1], arrived[2]))
    arrived += [lax.ppermute(part, "ctx", pairs) for part, pairs in zip(last, partners[n - 2 :])]
    col_feat = col_query.shape[1]
    col_results = unpacked(where, first, None, 0, col_feat, [])
    for some in (list(range(n - 2)), [n - 2, n - 1]):
        col_results = unpacked(
            where, [arrived[k] for k in some], some, half * HEAD_DIM, col_feat, col_results
        )

    outer_v = jnp.where(is_far, second_hop(hop), outer_v)
    row_grads = []
    for own, near, across in ((own_k, inner[0], outer_k), (own_v, inner[1], outer_v)):
        lo = jnp.where(odd == 1, near, across).astype(own.dtype)
        hi = jnp.where(odd == 1, across, near).astype(own.dtype)
        gap = jnp.zeros((tokens - rim, feat), own.dtype)
        added = jnp.concatenate([lo, gap]) + jnp.concatenate([gap, hi])
        row_grads.append((own + added).astype(jnp.bfloat16))
    return (
        row_output, row_dquery, *row_grads,
        *col_results,
    )


def solution(mesh):
    tokens, whole = P("ctx", "head"), P()
    return jax.shard_map(
        body,
        mesh=mesh,
        in_specs=(tokens,) * 4 + (whole,) + (tokens,) * 4 + (whole,),
        out_specs=(tokens,) * 8,
        check_vma=False,
    )
```

```python
import functools

import jax
import jax.numpy as jnp
import numpy as np
from jax import lax
from jax.experimental import pallas as pl
from jax.experimental.pallas import tpu as pltpu
from jax.sharding import PartitionSpec as P

HEAD_DIM = 128
GRIDC = 128
GROUP = 8
MASKED = -1e30
SCALE = HEAD_DIM**-0.5
EXP2_SCALE = SCALE * float(np.log2(np.e))
VMEM = 60 << 20
CHIPS_APART = 4


def contract(a, b, dim_a, dim_b):
    return lax.dot_general(
        a, b, (((dim_a,), (dim_b,)), ((), ())), preferred_element_type=jnp.float32
    )


def attend(queries, cotangent, keys, values, add_bias):
    n_keys, n_queries = keys.shape[0], queries.shape[0]
    scores = add_bias(contract(keys, queries, 1, 1))
    top = jnp.max(scores, axis=0, keepdims=True)
    terms = jnp.exp2((scores - top) * EXP2_SCALE)
    prob = terms * (1.0 / jnp.sum(terms, axis=0, keepdims=True))
    prob_low = prob.astype(jnp.bfloat16)
    output = contract(prob_low, values, 0, 0).astype(jnp.bfloat16)
    product = cotangent.astype(jnp.float32) * output.astype(jnp.float32)
    delta = jnp.sum(product.T, axis=0, keepdims=True)
    d_prob = contract(values, cotangent, 1, 1)
    d_scores = (prob * (d_prob - delta)).astype(jnp.bfloat16)
    grad_query = (contract(d_scores, keys, 0, 0) * SCALE).astype(jnp.bfloat16)
    grad_keys = contract(d_scores, queries, 1, 0)
    grad_values = contract(prob_low, cotangent, 1, 0)
    return output, grad_query, grad_keys, grad_values


def row_kernel(
    band, place, mask, q, k, v, d, inner_kv, outer_k, outer_v, far_v,
    out, dq, dk, dv, inner_grads, outer_dk, outer_dv, keys, values, acc_k, acc_v,
):
    tokens = q.shape[0]
    rim = outer_k.shape[0]
    odd_device = place[1]
    inner = pl.ds(pl.multiple_of((1 - odd_device) * (rim + tokens), GRIDC), rim)
    outer = pl.ds(pl.multiple_of(odd_device * (rim + tokens), GRIDC), rim)
    keys[rim : rim + tokens] = k[...]
    values[rim : rim + tokens] = v[...]
    keys[inner] = inner_kv[0]
    values[inner] = inner_kv[1]
    keys[outer] = outer_k[...]

    @pl.when(place[2] == 0)
    def _():
        values[outer] = outer_v[...]

    @pl.when(place[2] == 1)
    def _():
        values[outer] = far_v[...]

    acc_k[...] = jnp.zeros_like(acc_k)
    acc_v[...] = jnp.zeros_like(acc_v)
    blocks = 2 * band + 2
    odd = lax.broadcasted_iota(jnp.int32, (1, 2 * GRIDC), 1) >= GRIDC
    total = mask.shape[0]

    def block_bias(row, block):
        key_row = row - band + block
        inside = (key_row >= 0) & (key_row < total)
        sides = []
        for side in range(2):
            offset = block - side
            seen = inside & (mask[row + side, offset] == 1) if 0 <= offset <= 2 * band else False
            sides.append(jnp.where(seen, 0.0, MASKED).astype(jnp.float32))
        return jnp.where(odd, sides[1], sides[0])

    for pair in range(tokens // (2 * GRIDC)):
        here = pl.ds(pair * 2 * GRIDC, 2 * GRIDC)
        window = pl.ds(pair * 2 * GRIDC, blocks * GRIDC)

        def add_bias(scores):
            return jnp.concatenate(
                [
                    scores[b * GRIDC : (b + 1) * GRIDC] + block_bias(place[0] + 2 * pair, b)
                    for b in range(blocks)
                ],
                axis=0,
            )

        output, grad_query, grad_keys, grad_values = attend(
            q[here], d[here], keys[window], values[window], add_bias
        )
        out[here] = output
        dq[here] = grad_query
        acc_k[window] += grad_keys
        acc_v[window] += grad_values
    sides = ((acc_k, dk, outer_dk, SCALE), (acc_v, dv, outer_dv, 1.0))
    for at, (acc, own, across, factor) in enumerate(sides):
        own[...] = acc[rim : rim + tokens] * factor
        inner_grads[at] = (acc[inner] * factor).astype(across.dtype)
        across[...] = (acc[outer] * factor).astype(across.dtype)


def row_attention(place, mask, q, k, v, d, halos, band):
    tokens, feat = q.shape
    heads = feat // HEAD_DIM
    rim = band * GRIDC
    tall = pl.BlockSpec((tokens, HEAD_DIM), lambda h: (0, h))
    edge = pl.BlockSpec((rim, HEAD_DIM), lambda h: (0, h))
    both = pl.BlockSpec((2, rim, HEAD_DIM), lambda h: (0, 0, h))
    scalars = pl.BlockSpec(memory_space=pltpu.SMEM)
    padded = tokens + 2 * rim
    pairs = tokens * (2 * band + 2) * GRIDC * heads
    return pl.pallas_call(
        functools.partial(row_kernel, band),
        grid=(heads,),
        in_specs=[scalars, scalars, tall, tall, tall, tall, both, edge, edge, edge],
        out_specs=[tall] * 4 + [both, edge, edge],
        out_shape=[
            jax.ShapeDtypeStruct(q.shape, jnp.bfloat16),
            jax.ShapeDtypeStruct(q.shape, jnp.bfloat16),
            jax.ShapeDtypeStruct(q.shape, jnp.float32),
            jax.ShapeDtypeStruct(q.shape, jnp.float32),
            jax.ShapeDtypeStruct((2, rim, feat), jnp.bfloat16),
            jax.ShapeDtypeStruct((rim, feat), jnp.bfloat16),
            jax.ShapeDtypeStruct((rim, feat), jnp.bfloat16),
        ],
        scratch_shapes=[
            pltpu.VMEM((padded, HEAD_DIM), jnp.bfloat16),
            pltpu.VMEM((padded, HEAD_DIM), jnp.bfloat16),
            pltpu.VMEM((padded, HEAD_DIM), jnp.float32),
            pltpu.VMEM((padded, HEAD_DIM), jnp.float32),
        ],
        compiler_params=pltpu.CompilerParams(vmem_limit_bytes=VMEM),
        cost_estimate=pl.CostEstimate(
            flops=240 * pairs * HEAD_DIM, bytes_accessed=30 * tokens * feat, transcendentals=pairs
        ),
        name="row_heads",
    )(place, mask, q, k, v, d, *halos)


def col_kernel(n_parts, me, mask, x, earlier, *refs):
    outs, result, bias = refs[:n_parts], refs[n_parts], refs[-1]
    del earlier

    @pl.when((pl.program_id(0) == 0) & (pl.program_id(1) == 0))
    def _():
        size, total = bias.shape[0], mask.shape[0]
        row_of = lax.broadcasted_iota(jnp.int32, (size, total), 0) // GROUP
        spread = (row_of == lax.broadcasted_iota(jnp.int32, (size, total), 1)).astype(jnp.bfloat16)
        seen = (mask[...] == 1).astype(jnp.bfloat16)
        by_key = contract(spread, seen, 1, 1).astype(jnp.bfloat16)
        allowed = contract(by_key, spread, 1, 1)
        key_col = lax.broadcasted_iota(jnp.int32, (size, size), 0) % GROUP
        query_col = lax.broadcasted_iota(jnp.int32, (size, size), 1) % GROUP
        bias[...] = jnp.where((key_col == query_col) & (allowed > 0.5), 0.0, MASKED)

    shape = (x.shape[0], *x.shape[2:])
    tokens = shape[0] * shape[1] * shape[2]
    q, k, v, d = (x[:, a].reshape(tokens, HEAD_DIM) for a in range(4))
    chunk = min(tokens, 256)
    grad_keys, grad_values = 0.0, 0.0
    outputs, grads = [], []
    for start in range(0, tokens, chunk):
        here = slice(start, start + chunk)
        output, grad_query, more_keys, more_values = attend(
            q[here], d[here], k, v, lambda s: s + bias[:, here]
        )
        grad_keys += more_keys
        grad_values += more_values
        outputs.append(output)
        grads.append(grad_query)
    result[:, 0] = jnp.concatenate(outputs, 0).reshape(shape)
    result[:, 1] = jnp.concatenate(grads, 0).reshape(shape)
    result[:, 2] = (grad_keys * SCALE).astype(jnp.bfloat16).reshape(shape)
    result[:, 3] = grad_values.astype(jnp.bfloat16).reshape(shape)
    for partner, out in enumerate(outs):
        out[...] = result[me[0] ^ partner]


def col_attention(me, mask, x, earlier, start, heads, in_parts):
    n, k, rows, cols, _ = x.shape
    n_parts = n if in_parts else 0
    tokens = n * rows * GROUP
    block = (k, rows, GROUP, HEAD_DIM)
    pairs = tokens * tokens * heads * (cols // GROUP)
    part = (k, rows, cols, heads * HEAD_DIM)
    if in_parts:
        out_specs = [pl.BlockSpec(block, lambda h, g: (0, 0, g, h))] * n
        out_shape = [jax.ShapeDtypeStruct(part, jnp.bfloat16)] * n
        held = [pltpu.VMEM((n, *block), jnp.bfloat16)]
    else:
        out_specs = pl.BlockSpec((n, *block), lambda h, g: (0, 0, 0, g, h))
        out_shape = jax.ShapeDtypeStruct((n, *part), jnp.bfloat16)
        held = []
    return pl.pallas_call(
        functools.partial(col_kernel, n_parts),
        grid=(heads, cols // GROUP),
        in_specs=[
            pl.BlockSpec(memory_space=pltpu.SMEM),
            pl.BlockSpec(mask.shape, lambda h, g: (0, 0)),
            pl.BlockSpec((n, *block), lambda h, g: (0, 0, 0, g, h + start)),
            pl.BlockSpec(memory_space=pl.ANY),
        ],
        out_specs=out_specs,
        out_shape=out_shape,
        scratch_shapes=held + [pltpu.VMEM((tokens, tokens), jnp.float32)],
        compiler_params=pltpu.CompilerParams(vmem_limit_bytes=VMEM),
        cost_estimate=pl.CostEstimate(
            flops=240 * pairs * HEAD_DIM, bytes_accessed=4 * x.size, transcendentals=pairs
        ),
        name="col_heads",
    )(me, mask, x, earlier)


def pack_kernel(n, *refs):
    *parts, out, held, arrived, left = refs
    cols = GRIDC // n
    loads = [
        pltpu.make_async_copy(part, held.at[a], arrived.at[a]) for a, part in enumerate(parts)
    ]
    stores = [
        [
            pltpu.make_async_copy(
                held.at[a, :, j * cols : (j + 1) * cols, :], out.at[j, a], left.at[a, j]
            )
            for j in range(n)
        ]
        for a in range(len(parts))
    ]
    for load in loads:
        load.start()
    for load, several in zip(loads, stores):
        load.wait()
        for store in several:
            store.start()
    for several in stores:
        for store in several:
            store.wait()


def packed(arrays, n):
    tokens, feat = arrays[0].shape
    rows, cols, k = tokens // GRIDC, GRIDC // n, len(arrays)
    return pl.pallas_call(
        functools.partial(pack_kernel, n),
        in_specs=[pl.BlockSpec(memory_space=pl.ANY)] * k,
        out_specs=pl.BlockSpec(memory_space=pl.ANY),
        out_shape=jax.ShapeDtypeStruct((n, k, rows, cols, feat), jnp.bfloat16),
        scratch_shapes=[
            pltpu.VMEM((k, rows, GRIDC, feat), jnp.bfloat16),
            pltpu.SemaphoreType.DMA((k,)),
            pltpu.SemaphoreType.DMA((k, n)),
        ],
        compiler_params=pltpu.CompilerParams(vmem_limit_bytes=VMEM),
        cost_estimate=pl.CostEstimate(
            flops=0, bytes_accessed=4 * k * tokens * feat, transcendentals=0
        ),
        name="pack",
    )(*(a.reshape(rows, GRIDC, feat) for a in arrays))


def unpack_kernel(partners, start, me, *refs):
    held, arrived, left = refs[-3:]
    count, k, _, cols, width = held.shape
    outs = refs[-3 - k : -3]
    loads, stores = [], []
    for i in range(count):
        part, source = (refs[0].at[i], i) if partners is None else (refs[i], me[0] ^ partners[i])
        here = pl.ds(pl.multiple_of(source * cols, cols), cols)
        loads.append(pltpu.make_async_copy(part, held.at[i], arrived.at[i]))
        stores += [
            pltpu.make_async_copy(
                held.at[i, a], out.at[:, here, start : start + width], left.at[i, a]
            )
            for a, out in enumerate(outs)
        ]
    for load in loads:
        load.start()
    for i, load in enumerate(loads):
        load.wait()
        for store in stores[i * k : (i + 1) * k]:
            store.start()
    for store in stores:
        store.wait()


def unpacked(me, parts, partners, start, feat, kept):
    parts = [parts] if partners is None else parts
    k, rows, cols, width = parts[0].shape[-4:]
    count = GRIDC // cols if partners is None else len(parts)
    kept = [a.reshape(rows, GRIDC, feat) for a in kept]
    outs = pl.pallas_call(
        functools.partial(unpack_kernel, partners, start),
        in_specs=[pl.BlockSpec(memory_space=pltpu.SMEM)]
        + [pl.BlockSpec(memory_space=pl.ANY)] * (len(parts) + len(kept)),
        out_specs=[pl.BlockSpec(memory_space=pl.ANY)] * k,
        out_shape=[jax.ShapeDtypeStruct((rows, GRIDC, feat), jnp.bfloat16)] * k,
        scratch_shapes=[
            pltpu.VMEM((count, k, rows, cols, width), jnp.bfloat16),
            pltpu.SemaphoreType.DMA((count,)),
            pltpu.SemaphoreType.DMA((count, k)),
        ],
        input_output_aliases={1 + len(parts) + a: a for a in range(len(kept))},
        compiler_params=pltpu.CompilerParams(vmem_limit_bytes=VMEM),
        cost_estimate=pl.CostEstimate(
            flops=0, bytes_accessed=4 * k * rows * count * cols * width, transcendentals=0
        ),
        name="unpack",
    )(me, *parts, *kept)
    return [o.reshape(rows * GRIDC, feat) for o in outs]


def swapped(inner, outer_k, outer_v):
    n = lax.axis_size("ctx")
    across = [(i, i + 1) for i in range(1, n - 1, 2)]
    far = [(i, j) for i, j in across if j % CHIPS_APART == 0 and j + CHIPS_APART <= n]
    near = [pair for pair in across if pair not in far]
    back = lambda pairs: [(j, i) for i, j in pairs]
    step = CHIPS_APART
    first = [(i, i + step) for i, _ in far] + [(j, j - step) for _, j in far]
    second = [(i + step, j) for i, j in far] + [(j - step, i) for i, j in far]
    outer_v = lax.ppermute(outer_v, "ctx", near + back(near) + first)
    outer_k = lax.ppermute(outer_k, "ctx", across + back(across))
    inner = lax.ppermute(inner, "ctx", [(i, i ^ 1) for i in range(n)])
    return inner, outer_k, outer_v, lambda passed: lax.ppermute(passed, "ctx", second)


def handed_back(inner, outer_k, outer_v):
    n = lax.axis_size("ctx")
    across = [(i, i + 1) for i in range(1, n - 1, 2)]
    pairs = across + [(j, i) for i, j in across]
    inner = lax.ppermute(inner, "ctx", [(i, i ^ 1) for i in range(n)])
    return inner, lax.ppermute(outer_k, "ctx", pairs), lax.ppermute(outer_v, "ctx", pairs)


def exchanged(x):
    return lax.all_to_all(x, "ctx", 0, 0, tiled=True)


def body(
    row_query, row_key, row_value, row_cotangent, row_mask,
    col_query, col_key, col_value, col_cotangent, col_mask,
):
    n = lax.axis_size("ctx")
    tokens = row_query.shape[0]
    rows = tokens // GRIDC
    band = (row_mask.shape[1] - 1) // 2
    rim = band * GRIDC

    feat = row_key.shape[1]
    me = lax.axis_index("ctx")
    odd = me % 2
    side = me % CHIPS_APART
    inner_at, outer_at = (1 - odd) * (tokens - rim), odd * (tokens - rim)
    rim_of = lambda x, at: lax.dynamic_slice_in_dim(x, at, rim, 0)
    inner = jnp.stack([rim_of(row_key, inner_at), rim_of(row_value, inner_at)])
    outer_k, outer_v = rim_of(row_key, outer_at), rim_of(row_value, outer_at)
    cols = [col_query, col_key, col_value, col_cotangent]
    inner, outer_k, outer_v, cols = lax.optimization_barrier((inner, outer_k, outer_v, cols))
    inner, outer_k, outer_v, second_hop = swapped(inner, outer_k, outer_v)
    sent, outer_v = lax.optimization_barrier((packed(cols, n), outer_v))
    halos = [inner, outer_k, outer_v, second_hop(outer_v)]
    moved = exchanged(sent)

    is_far = (side == 0) | (side == CHIPS_APART - 1)
    place = jnp.stack([me * rows, odd, is_far.astype(odd.dtype)])
    row_output, row_dquery, own_k, own_v, *sides = row_attention(
        place, row_mask, row_query, row_key, row_value, row_cotangent, halos, band
    )
    inner, outer_k, outer_v = handed_back(*sides)

    heads = col_query.shape[1] // HEAD_DIM
    half = heads // 2
    where = me.reshape(1)
    partners = [[(i, i ^ k) for i in range(n)] for k in range(n)]
    first = col_attention(where, col_mask, moved, row_output, 0, half, False)
    first, inner, outer_k = lax.optimization_barrier((first, inner, outer_k))
    second = col_attention(where, col_mask, moved, first, half, heads - half, True)
    second, outer_v = lax.optimization_barrier((second, outer_v))
    first = exchanged(first)
    arrived = [second[0]] + [
        lax.ppermute(second[k], "ctx", partners[k]) for k in range(1, n - 2)
    ]
    *last, arrived[1] = lax.optimization_barrier((second[n - 2], second[n - 1], arrived[1]))
    arrived += [lax.ppermute(part, "ctx", pairs) for part, pairs in zip(last, partners[n - 2 :])]
    col_feat = col_query.shape[1]
    col_results = unpacked(where, first, None, 0, col_feat, [])
    for some in (list(range(n - 2)), [n - 2, n - 1]):
        col_results = unpacked(
            where, [arrived[k] for k in some], some, half * HEAD_DIM, col_feat, col_results
        )

    row_grads = []
    for own, near, across in ((own_k, inner[0], outer_k), (own_v, inner[1], outer_v)):
        lo = jnp.where(odd == 1, near, across).astype(own.dtype)
        hi = jnp.where(odd == 1, across, near).astype(own.dtype)
        gap = jnp.zeros((tokens - rim, feat), own.dtype)
        added = jnp.concatenate([lo, gap]) + jnp.concatenate([gap, hi])
        row_grads.append((own + added).astype(jnp.bfloat16))
    return (
        row_output, row_dquery, *row_grads,
        *col_results,
    )


def solution(mesh):
    tokens, whole = P("ctx", "head"), P()
    return jax.shard_map(
        body,
        mesh=mesh,
        in_specs=(tokens,) * 4 + (whole,) + (tokens,) * 4 + (whole,),
        out_specs=(tokens,) * 8,
        check_vma=False,
    )
```

```python
import functools

import jax
import jax.numpy as jnp
import numpy as np
from jax import lax
from jax.experimental import pallas as pl
from jax.experimental.pallas import tpu as pltpu
from jax.sharding import PartitionSpec as P

HEAD_DIM = 128
GRIDC = 128
GROUP = 8
MASKED = -1e30
SCALE = HEAD_DIM**-0.5
EXP2_SCALE = SCALE * float(np.log2(np.e))
VMEM = 60 << 20
CHIPS_APART = 4


def contract(a, b, dim_a, dim_b):
    return lax.dot_general(
        a, b, (((dim_a,), (dim_b,)), ((), ())), preferred_element_type=jnp.float32
    )


def attend(queries, cotangent, keys, values, add_bias):
    n_keys, n_queries = keys.shape[0], queries.shape[0]
    scores = add_bias(contract(keys, queries, 1, 1))
    top = jnp.max(scores, axis=0, keepdims=True)
    terms = jnp.exp2((scores - top) * EXP2_SCALE)
    prob = terms * (1.0 / jnp.sum(terms, axis=0, keepdims=True))
    prob_low = prob.astype(jnp.bfloat16)
    output = contract(prob_low, values, 0, 0).astype(jnp.bfloat16)
    product = cotangent.astype(jnp.float32) * output.astype(jnp.float32)
    delta = jnp.sum(product.T, axis=0, keepdims=True)
    d_prob = contract(values, cotangent, 1, 1)
    d_scores = (prob * (d_prob - delta)).astype(jnp.bfloat16)
    grad_query = (contract(d_scores, keys, 0, 0) * SCALE).astype(jnp.bfloat16)
    grad_keys = contract(d_scores, queries, 1, 0)
    grad_values = contract(prob_low, cotangent, 1, 0)
    return output, grad_query, grad_keys, grad_values


def row_kernel(
    band, place, mask, q, k, v, d, inner_kv, outer_k, outer_v, far_v,
    out, dq, dk, dv, inner_grads, outer_dk, outer_dv, keys, values, acc_k, acc_v,
):
    tokens = q.shape[0]
    rim = outer_k.shape[0]
    odd_device = place[1]
    inner = pl.ds(pl.multiple_of((1 - odd_device) * (rim + tokens), GRIDC), rim)
    outer = pl.ds(pl.multiple_of(odd_device * (rim + tokens), GRIDC), rim)
    keys[rim : rim + tokens] = k[...]
    values[rim : rim + tokens] = v[...]
    keys[inner] = inner_kv[0]
    values[inner] = inner_kv[1]
    keys[outer] = outer_k[...]

    @pl.when(place[2] == 0)
    def _():
        values[outer] = outer_v[...]

    @pl.when(place[2] == 1)
    def _():
        values[outer] = far_v[...]

    acc_k[...] = jnp.zeros_like(acc_k)
    acc_v[...] = jnp.zeros_like(acc_v)
    blocks = 2 * band + 2
    odd = lax.broadcasted_iota(jnp.int32, (1, 2 * GRIDC), 1) >= GRIDC
    total = mask.shape[0]

    def block_bias(row, block):
        key_row = row - band + block
        inside = (key_row >= 0) & (key_row < total)
        sides = []
        for side in range(2):
            offset = block - side
            seen = inside & (mask[row + side, offset] == 1) if 0 <= offset <= 2 * band else False
            sides.append(jnp.where(seen, 0.0, MASKED).astype(jnp.float32))
        return jnp.where(odd, sides[1], sides[0])

    for pair in range(tokens // (2 * GRIDC)):
        here = pl.ds(pair * 2 * GRIDC, 2 * GRIDC)
        window = pl.ds(pair * 2 * GRIDC, blocks * GRIDC)

        def add_bias(scores):
            return jnp.concatenate(
                [
                    scores[b * GRIDC : (b + 1) * GRIDC] + block_bias(place[0] + 2 * pair, b)
                    for b in range(blocks)
                ],
                axis=0,
            )

        output, grad_query, grad_keys, grad_values = attend(
            q[here], d[here], keys[window], values[window], add_bias
        )
        out[here] = output
        dq[here] = grad_query
        acc_k[window] += grad_keys
        acc_v[window] += grad_values
    sides = ((acc_k, dk, outer_dk, SCALE), (acc_v, dv, outer_dv, 1.0))
    for at, (acc, own, across, factor) in enumerate(sides):
        own[...] = acc[rim : rim + tokens] * factor
        inner_grads[at] = (acc[inner] * factor).astype(across.dtype)
        across[...] = (acc[outer] * factor).astype(across.dtype)


def row_attention(place, mask, q, k, v, d, halos, band):
    tokens, feat = q.shape
    heads = feat // HEAD_DIM
    rim = band * GRIDC
    tall = pl.BlockSpec((tokens, HEAD_DIM), lambda h: (0, h))
    edge = pl.BlockSpec((rim, HEAD_DIM), lambda h: (0, h))
    both = pl.BlockSpec((2, rim, HEAD_DIM), lambda h: (0, 0, h))
    scalars = pl.BlockSpec(memory_space=pltpu.SMEM)
    padded = tokens + 2 * rim
    pairs = tokens * (2 * band + 2) * GRIDC * heads
    return pl.pallas_call(
        functools.partial(row_kernel, band),
        grid=(heads,),
        in_specs=[scalars, scalars, tall, tall, tall, tall, both, edge, edge, edge],
        out_specs=[tall] * 4 + [both, edge, edge],
        out_shape=[
            jax.ShapeDtypeStruct(q.shape, jnp.bfloat16),
            jax.ShapeDtypeStruct(q.shape, jnp.bfloat16),
            jax.ShapeDtypeStruct(q.shape, jnp.float32),
            jax.ShapeDtypeStruct(q.shape, jnp.float32),
            jax.ShapeDtypeStruct((2, rim, feat), jnp.bfloat16),
            jax.ShapeDtypeStruct((rim, feat), jnp.bfloat16),
            jax.ShapeDtypeStruct((rim, feat), jnp.bfloat16),
        ],
        scratch_shapes=[
            pltpu.VMEM((padded, HEAD_DIM), jnp.bfloat16),
            pltpu.VMEM((padded, HEAD_DIM), jnp.bfloat16),
            pltpu.VMEM((padded, HEAD_DIM), jnp.float32),
            pltpu.VMEM((padded, HEAD_DIM), jnp.float32),
        ],
        compiler_params=pltpu.CompilerParams(vmem_limit_bytes=VMEM),
        cost_estimate=pl.CostEstimate(
            flops=240 * pairs * HEAD_DIM, bytes_accessed=30 * tokens * feat, transcendentals=pairs
        ),
        name="row_heads",
    )(place, mask, q, k, v, d, *halos)


def col_kernel(n_parts, me, mask, x, earlier, *refs):
    outs, result, bias = refs[:n_parts], refs[n_parts], refs[-1]
    del earlier

    @pl.when((pl.program_id(0) == 0) & (pl.program_id(1) == 0))
    def _():
        size, total = bias.shape[0], mask.shape[0]
        row_of = lax.broadcasted_iota(jnp.int32, (size, total), 0) // GROUP
        spread = (row_of == lax.broadcasted_iota(jnp.int32, (size, total), 1)).astype(jnp.bfloat16)
        seen = (mask[...] == 1).astype(jnp.bfloat16)
        by_key = contract(spread, seen, 1, 1).astype(jnp.bfloat16)
        allowed = contract(by_key, spread, 1, 1)
        key_col = lax.broadcasted_iota(jnp.int32, (size, size), 0) % GROUP
        query_col = lax.broadcasted_iota(jnp.int32, (size, size), 1) % GROUP
        bias[...] = jnp.where((key_col == query_col) & (allowed > 0.5), 0.0, MASKED)

    shape = (x.shape[0], *x.shape[2:])
    tokens = shape[0] * shape[1] * shape[2]
    q, k, v, d = (x[:, a].reshape(tokens, HEAD_DIM) for a in range(4))
    chunk = min(tokens, 256)
    grad_keys, grad_values = 0.0, 0.0
    outputs, grads = [], []
    for start in range(0, tokens, chunk):
        here = slice(start, start + chunk)
        output, grad_query, more_keys, more_values = attend(
            q[here], d[here], k, v, lambda s: s + bias[:, here]
        )
        grad_keys += more_keys
        grad_values += more_values
        outputs.append(output)
        grads.append(grad_query)
    result[:, 0] = jnp.concatenate(outputs, 0).reshape(shape)
    result[:, 1] = jnp.concatenate(grads, 0).reshape(shape)
    result[:, 2] = (grad_keys * SCALE).astype(jnp.bfloat16).reshape(shape)
    result[:, 3] = grad_values.astype(jnp.bfloat16).reshape(shape)
    for partner, out in enumerate(outs):
        out[...] = result[me[0] ^ partner]


def col_attention(me, mask, x, earlier, start, heads, in_parts):
    n, k, rows, cols, _ = x.shape
    n_parts = n if in_parts else 0
    tokens = n * rows * GROUP
    block = (k, rows, GROUP, HEAD_DIM)
    pairs = tokens * tokens * heads * (cols // GROUP)
    part = (k, rows, cols, heads * HEAD_DIM)
    if in_parts:
        out_specs = [pl.BlockSpec(block, lambda h, g: (0, 0, g, h))] * n
        out_shape = [jax.ShapeDtypeStruct(part, jnp.bfloat16)] * n
        held = [pltpu.VMEM((n, *block), jnp.bfloat16)]
    else:
        out_specs = pl.BlockSpec((n, *block), lambda h, g: (0, 0, 0, g, h))
        out_shape = jax.ShapeDtypeStruct((n, *part), jnp.bfloat16)
        held = []
    return pl.pallas_call(
        functools.partial(col_kernel, n_parts),
        grid=(heads, cols // GROUP),
        in_specs=[
            pl.BlockSpec(memory_space=pltpu.SMEM),
            pl.BlockSpec(mask.shape, lambda h, g: (0, 0)),
            pl.BlockSpec((n, *block), lambda h, g: (0, 0, 0, g, h + start)),
            pl.BlockSpec(memory_space=pl.ANY),
        ],
        out_specs=out_specs,
        out_shape=out_shape,
        scratch_shapes=held + [pltpu.VMEM((tokens, tokens), jnp.float32)],
        compiler_params=pltpu.CompilerParams(vmem_limit_bytes=VMEM),
        cost_estimate=pl.CostEstimate(
            flops=240 * pairs * HEAD_DIM, bytes_accessed=4 * x.size, transcendentals=pairs
        ),
        name="col_heads",
    )(me, mask, x, earlier)


def pack_kernel(n, *refs):
    *parts, out, held, arrived, left = refs
    cols = GRIDC // n
    loads = [
        pltpu.make_async_copy(part, held.at[a], arrived.at[a]) for a, part in enumerate(parts)
    ]
    stores = [
        [
            pltpu.make_async_copy(
                held.at[a, :, j * cols : (j + 1) * cols, :], out.at[j, a], left.at[a, j]
            )
            for j in range(n)
        ]
        for a in range(len(parts))
    ]
    for load in loads:
        load.start()
    for load, several in zip(loads, stores):
        load.wait()
        for store in several:
            store.start()
    for several in stores:
        for store in several:
            store.wait()


def packed(arrays, n):
    tokens, feat = arrays[0].shape
    rows, cols, k = tokens // GRIDC, GRIDC // n, len(arrays)
    return pl.pallas_call(
        functools.partial(pack_kernel, n),
        in_specs=[pl.BlockSpec(memory_space=pl.ANY)] * k,
        out_specs=pl.BlockSpec(memory_space=pl.ANY),
        out_shape=jax.ShapeDtypeStruct((n, k, rows, cols, feat), jnp.bfloat16),
        scratch_shapes=[
            pltpu.VMEM((k, rows, GRIDC, feat), jnp.bfloat16),
            pltpu.SemaphoreType.DMA((k,)),
            pltpu.SemaphoreType.DMA((k, n)),
        ],
        compiler_params=pltpu.CompilerParams(vmem_limit_bytes=VMEM),
        cost_estimate=pl.CostEstimate(
            flops=0, bytes_accessed=4 * k * tokens * feat, transcendentals=0
        ),
        name="pack",
    )(*(a.reshape(rows, GRIDC, feat) for a in arrays))


def unpack_kernel(partners, start, me, *refs):
    held, arrived, left = refs[-3:]
    count, k, _, cols, width = held.shape
    outs = refs[-3 - k : -3]
    loads, stores = [], []
    for i in range(count):
        part, source = (refs[0].at[i], i) if partners is None else (refs[i], me[0] ^ partners[i])
        here = pl.ds(pl.multiple_of(source * cols, cols), cols)
        loads.append(pltpu.make_async_copy(part, held.at[i], arrived.at[i]))
        stores += [
            pltpu.make_async_copy(
                held.at[i, a], out.at[:, here, start : start + width], left.at[i, a]
            )
            for a, out in enumerate(outs)
        ]
    for load in loads:
        load.start()
    for i, load in enumerate(loads):
        load.wait()
        for store in stores[i * k : (i + 1) * k]:
            store.start()
    for store in stores:
        store.wait()


def unpacked(me, parts, partners, start, feat, kept):
    parts = [parts] if partners is None else parts
    k, rows, cols, width = parts[0].shape[-4:]
    count = GRIDC // cols if partners is None else len(parts)
    kept = [a.reshape(rows, GRIDC, feat) for a in kept]
    outs = pl.pallas_call(
        functools.partial(unpack_kernel, partners, start),
        in_specs=[pl.BlockSpec(memory_space=pltpu.SMEM)]
        + [pl.BlockSpec(memory_space=pl.ANY)] * (len(parts) + len(kept)),
        out_specs=[pl.BlockSpec(memory_space=pl.ANY)] * k,
        out_shape=[jax.ShapeDtypeStruct((rows, GRIDC, feat), jnp.bfloat16)] * k,
        scratch_shapes=[
            pltpu.VMEM((count, k, rows, cols, width), jnp.bfloat16),
            pltpu.SemaphoreType.DMA((count,)),
            pltpu.SemaphoreType.DMA((count, k)),
        ],
        input_output_aliases={1 + len(parts) + a: a for a in range(len(kept))},
        compiler_params=pltpu.CompilerParams(vmem_limit_bytes=VMEM),
        cost_estimate=pl.CostEstimate(
            flops=0, bytes_accessed=4 * k * rows * count * cols * width, transcendentals=0
        ),
        name="unpack",
    )(me, *parts, *kept)
    return [o.reshape(rows * GRIDC, feat) for o in outs]


def swapped(inner, outer_k, outer_v):
    n = lax.axis_size("ctx")
    across = [(i, i + 1) for i in range(1, n - 1, 2)]
    far = [(i, j) for i, j in across if j % CHIPS_APART == 0 and j + CHIPS_APART <= n]
    near = [pair for pair in across if pair not in far]
    back = lambda pairs: [(j, i) for i, j in pairs]
    step = CHIPS_APART
    first = [(i, i + step) for i, _ in far] + [(j, j - step) for _, j in far]
    second = [(i + step, j) for i, j in far] + [(j - step, i) for i, j in far]
    outer_v = lax.ppermute(outer_v, "ctx", near + back(near) + first)
    outer_k = lax.ppermute(outer_k, "ctx", across + back(across))
    inner = lax.ppermute(inner, "ctx", [(i, i ^ 1) for i in range(n)])
    return inner, outer_k, outer_v, lambda passed: lax.ppermute(passed, "ctx", second)


def handed_back(inner, outer_k, outer_v):
    n = lax.axis_size("ctx")
    across = [(i, i + 1) for i in range(1, n - 1, 2)]
    pairs = across + [(j, i) for i, j in across]
    inner = lax.ppermute(inner, "ctx", [(i, i ^ 1) for i in range(n)])
    return inner, lax.ppermute(outer_k, "ctx", pairs), lax.ppermute(outer_v, "ctx", pairs)


def exchanged(x):
    return lax.all_to_all(x, "ctx", 0, 0, tiled=True)


def body(
    row_query, row_key, row_value, row_cotangent, row_mask,
    col_query, col_key, col_value, col_cotangent, col_mask,
):
    n = lax.axis_size("ctx")
    tokens = row_query.shape[0]
    rows = tokens // GRIDC
    band = (row_mask.shape[1] - 1) // 2
    rim = band * GRIDC

    feat = row_key.shape[1]
    me = lax.axis_index("ctx")
    odd = me % 2
    side = me % CHIPS_APART
    inner_at, outer_at = (1 - odd) * (tokens - rim), odd * (tokens - rim)
    rim_of = lambda x, at: lax.dynamic_slice_in_dim(x, at, rim, 0)
    inner = jnp.stack([rim_of(row_key, inner_at), rim_of(row_value, inner_at)])
    outer_k, outer_v = rim_of(row_key, outer_at), rim_of(row_value, outer_at)
    cols = [col_query, col_key, col_value, col_cotangent]
    inner, outer_k, outer_v, cols = lax.optimization_barrier((inner, outer_k, outer_v, cols))
    inner, outer_k, outer_v, second_hop = swapped(inner, outer_k, outer_v)
    sent, outer_v = lax.optimization_barrier((packed(cols, n), outer_v))
    halos = [inner, outer_k, outer_v, second_hop(outer_v)]
    moved = exchanged(sent)

    is_far = (side == 0) | (side == CHIPS_APART - 1)
    place = jnp.stack([me * rows, odd, is_far.astype(odd.dtype)])
    row_output, row_dquery, own_k, own_v, *sides = row_attention(
        place, row_mask, row_query, row_key, row_value, row_cotangent, halos, band
    )
    inner, outer_k, outer_v = handed_back(*sides)

    heads = col_query.shape[1] // HEAD_DIM
    half = heads // 2
    where = me.reshape(1)
    partners = [[(i, i ^ k) for i in range(n)] for k in range(n)]
    first = col_attention(where, col_mask, moved, row_output, 0, half, False)
    first, inner, outer_v = lax.optimization_barrier((first, inner, outer_v))
    second = col_attention(where, col_mask, moved, first, half, heads - half, True)
    first = exchanged(first)
    arrived = [second[0]] + [
        lax.ppermute(second[k], "ctx", partners[k]) for k in range(1, n - 1)
    ]
    last, arrived[1] = lax.optimization_barrier((second[n - 1], arrived[1]))
    arrived.append(lax.ppermute(last, "ctx", partners[n - 1]))
    col_feat = col_query.shape[1]
    col_results = unpacked(where, first, None, 0, col_feat, [])
    for some in (list(range(n - 1)), [n - 1]):
        col_results = unpacked(
            where, [arrived[k] for k in some], some, half * HEAD_DIM, col_feat, col_results
        )

    row_grads = []
    for own, near, across in ((own_k, inner[0], outer_k), (own_v, inner[1], outer_v)):
        lo = jnp.where(odd == 1, near, across).astype(own.dtype)
        hi = jnp.where(odd == 1, across, near).astype(own.dtype)
        gap = jnp.zeros((tokens - rim, feat), own.dtype)
        added = jnp.concatenate([lo, gap]) + jnp.concatenate([gap, hi])
        row_grads.append((own + added).astype(jnp.bfloat16))
    return (
        row_output, row_dquery, *row_grads,
        *col_results,
    )


def solution(mesh):
    tokens, whole = P("ctx", "head"), P()
    return jax.shard_map(
        body,
        mesh=mesh,
        in_specs=(tokens,) * 4 + (whole,) + (tokens,) * 4 + (whole,),
        out_specs=(tokens,) * 8,
        check_vma=False,
    )
```
